256 devices in a mesh: face: 16 (over x_hi, y, core), band: 16 (over z, x_lo).
Axes of the slice: x: 4 (x_hi: 2, x_lo: 2; x = x_hi * 2 + x_lo), y: 4, z: 8, core: 2. Of those that a mesh axis runs over, the one named last changes fastest.
Arguments:
- coarse: bfloat16 [192, 256, 256], P('band', 'face'), may hold values from -6 to 6
- skip: bfloat16 [384, 512, 256], P('band', 'face'), may hold values from -6 to 6
- up_weight: bfloat16 [3, 3, 256, 256], replicated, may hold values from -0.25 to 0.25
- conv_weight: bfloat16 [3, 3, 256, 256], replicated, may hold values from -0.125 to 0.125
- cotangent: bfloat16 [384, 512, 256], P('band', 'face'), may hold values from -6 to 6
Outputs:
- decoded: bfloat16 [384, 512, 256], P('band', 'face')
- grad_coarse: bfloat16 [192, 256, 256], P('band', 'face')
- grad_up_weight: float32 [2304, 256], P('face', 'band')
- grad_conv_weight: float32 [2304, 256], P('face', 'band')
The draws below stay inside these ranges and needn't reach their ends.
All inputs are finite; a program needn't handle non-finite values.
Results may differ from the reference program's by a relative error of at most 0.0049.
Values may be sent and summed in bfloat16 or wider, within the bound.
A program may use at most 128 MiB of HBM per device.

```python
import jax
import jax.numpy as jnp

C = 256
H = 192
W = 256


def shard_levels(stream_key, shape, pieces, low, top_value):
    gain, own = 1.0, jax.random.fold_in(stream_key, 6)
    for dim, shards_of in pieces:
        steps = jnp.exp(jax.random.uniform(jax.random.fold_in(own, dim), (shards_of,), jnp.float32, low / len(pieces), top_value / len(pieces)))
        gain = gain * jnp.repeat(steps, shape[dim] // shards_of).reshape([-1 if axis == dim else 1 for axis in range(len(shape))])
    return gain


def centred(rng, dims, spread, bound, split=(), dtype=jnp.bfloat16):
    level = shard_levels(rng, dims, split, -0.22, 0.18) if split else 1.0
    values = jax.random.normal(rng, dims, jnp.float32) * spread * level
    return jnp.minimum(jnp.maximum(values, -bound), bound).astype(dtype)


def setup_inputs(seed: int = 0) -> dict:
    keys = jax.random.split(jax.random.key(seed), 6)
    coarse = centred(keys[0], (H, W, C), 1.0, 6.0, ((0, 16), (1, 16)))
    skip = centred(keys[1], (2 * H, 2 * W, C), 1.0, 6.0, ((0, 16), (1, 16)))
    up_weight = centred(keys[2], (3, 3, C, C), (2 * C) ** -0.5, 0.25)
    conv_weight = centred(keys[3], (3, 3, C, C), (9 * C) ** -0.5, 0.125)
    cotangent = centred(keys[4], (2 * H, 2 * W, C), 1.0, 6.0, ((0, 16), (1, 16)))
    return dict(coarse=coarse, skip=skip, up_weight=up_weight, conv_weight=conv_weight, cotangent=cotangent)


forward_taps = ((1, 1), (0, 0), (1, 0))
backward_taps = ((1, 0), (0, 1), (1, 1))

def up_phases(extended, up_weight, n_rows, n_cols):
    channels = extended.shape[-1]
    totals = {}
    for row_tap in range(3):
        row_phase, row_off = forward_taps[row_tap]
        for col_tap in range(3):
            col_phase, col_off = forward_taps[col_tap]
            source = extended[row_off:row_off + n_rows, col_off:col_off + n_cols].reshape(-1, channels)
            term = jnp.dot(source, up_weight[row_tap, col_tap], preferred_element_type=jnp.float32)
            name = (row_phase, col_phase)
            totals[name] = totals[name] + term if name in totals else term
    per_row = []
    for row_phase in range(2):
        per_row.append(jnp.stack([totals[row_phase, col_phase].reshape(n_rows, n_cols, channels) for col_phase in range(2)], axis=2))
    return jnp.stack(per_row, axis=1)

def conv_forward(act_pad, conv_weight, n_rows, n_cols):
    channels = act_pad.shape[-1]
    total = jnp.zeros((n_rows * n_cols, channels), jnp.float32)
    for row_tap in range(3):
        for col_tap in range(3):
            source = act_pad[row_tap:row_tap + n_rows, col_tap:col_tap + n_cols].reshape(-1, channels)
            total = total + jnp.dot(source, conv_weight[row_tap, col_tap], preferred_element_type=jnp.float32)
    return total

def conv_backward(grad_pad, conv_weight, n_rows, n_cols):
    channels = grad_pad.shape[-1]
    total = jnp.zeros((n_rows * n_cols, channels), jnp.float32)
    for row_tap in range(3):
        for col_tap in range(3):
            source = grad_pad[2 - row_tap:2 - row_tap + n_rows, 2 - col_tap:2 - col_tap + n_cols].reshape(-1, channels)
            total = total + jnp.dot(source, conv_weight[row_tap, col_tap].T, preferred_element_type=jnp.float32)
    return total

def conv_wgrad(act_pad, grad_flat, n_rows, n_cols):
    channels = act_pad.shape[-1]
    blocks = []
    for row_tap in range(3):
        for col_tap in range(3):
            source = act_pad[row_tap:row_tap + n_rows, col_tap:col_tap + n_cols].reshape(-1, channels)
            blocks.append(jnp.dot(source.T, grad_flat, preferred_element_type=jnp.float32))
    return jnp.concatenate(blocks, axis=0)

def down_backward(grad_ext, coarse, up_weight, n_rows, n_cols):
    channels = coarse.shape[-1]
    coarse_flat = coarse.reshape(-1, channels)
    grad_in = jnp.zeros((n_rows * n_cols, channels), jnp.float32)
    blocks = []
    for row_tap in range(3):
        row_phase, row_start = backward_taps[row_tap]
        for col_tap in range(3):
            col_phase, col_start = backward_taps[col_tap]
            source = grad_ext[row_start:row_start + n_rows, row_phase, col_start:col_start + n_cols, col_phase].reshape(-1, channels)
            grad_in = grad_in + jnp.dot(source, up_weight[row_tap, col_tap].T, preferred_element_type=jnp.float32)
            blocks.append(jnp.dot(coarse_flat.T, source, preferred_element_type=jnp.float32))
    return (grad_in, jnp.concatenate(blocks, axis=0))

def wrap_pad(field):
    widened = jnp.concatenate([field[:, -1:], field, field[:, :1]], axis=1)
    return jnp.pad(widened, ((1, 1), (0, 0), (0, 0)))

def reference(coarse, skip, up_weight, conv_weight, cotangent):
    n_rows, n_cols, channels = coarse.shape
    extended = jnp.concatenate([coarse, coarse[:, :1]], axis=1)
    extended = jnp.pad(extended, ((0, 1), (0, 0), (0, 0)))
    upsampled = up_phases(extended, up_weight, n_rows, n_cols).reshape(2 * n_rows, 2 * n_cols, channels)
    preact = upsampled + skip.astype(jnp.float32)
    act = jax.nn.silu(preact).astype(jnp.bfloat16)
    act_pad = wrap_pad(act)
    decoded = conv_forward(act_pad, conv_weight, 2 * n_rows, 2 * n_cols)
    decoded = decoded.reshape(2 * n_rows, 2 * n_cols, channels).astype(jnp.bfloat16)
    grad_pad = wrap_pad(cotangent)
    grad_act = conv_backward(grad_pad, conv_weight, 2 * n_rows, 2 * n_cols).reshape(2 * n_rows, 2 * n_cols, channels)
    sigma = jax.nn.sigmoid(preact)
    grad_pre = (grad_act * sigma * (1.0 + preact * (1.0 - sigma))).astype(jnp.bfloat16)
    phased = grad_pre.reshape(n_rows, 2, n_cols, 2, channels)
    widened_grad = jnp.concatenate([phased[:, :, -1:], phased], axis=2)
    grad_ext = jnp.pad(widened_grad, ((1, 0), (0, 0), (0, 0), (0, 0), (0, 0)))
    grad_in, grad_up = down_backward(grad_ext, coarse, up_weight, n_rows, n_cols)
    grad_conv = conv_wgrad(act_pad, cotangent.reshape(-1, channels), 2 * n_rows, 2 * n_cols)
    grad_coarse = grad_in.reshape(n_rows, n_cols, channels).astype(jnp.bfloat16)
    return (decoded, grad_coarse, grad_up, grad_conv)
```

```python
import functools

import jax
import jax.numpy as jnp
from jax import lax
from jax.experimental import pallas as pl
from jax.experimental.pallas import tpu as pltpu
from jax.sharding import PartitionSpec as P

F32, BF16 = jnp.float32, jnp.bfloat16
MESH = pl.DeviceIdType.MESH
CH = 256
RI, CJ = 12, 16
XR, XC = 18, 32
AREA = XR * XC

MSG_UP = (0, 1, 2, 5, 6)
MSG_DOWN = (0, 3, 4, 5, 6, 7, 8)
MSG_LEFT = (0, 1, 3, 5, 7)
MSG_RIGHT = (0, 2, 4, 5, 6, 7, 8)
CORNERS = (
    (-1, -1, (0, 1, 5)),
    (-1, 1, (0, 2, 5, 6)),
    (1, -1, (0, 3, 5, 7)),
    (1, 1, (0, 4, 5, 6, 7, 8)),
)
TAPS = [(k, l) for k in range(3) for l in range(3)]


def split(e):
    return e % 2, e // 2


def dot(a, b):
    return jnp.dot(a, b, preferred_element_type=F32)


def ld(ref, at, n, stride=1):
    if stride == 1:
        return jnp.concatenate([ref[h, pl.ds(at, n), :] for h in range(2)], axis=-1)
    return jnp.concatenate([ref[h, pl.ds(at, n, stride=stride), :] for h in range(2)], axis=-1)


def st(ref, at, n, value, stride=1):
    for h in range(2):
        part = value[:, 128 * h : 128 * h + 128]
        if stride == 1:
            ref[h, pl.ds(at, n), :] = part
        else:
            ref[h, pl.ds(at, n, stride=stride), :] = part


def kernel(
    dims,
    coarse_h, skip_h, upw_h, convw_h, cot_h,
    dec_h, gc_h, gu_o, gw_o,
    coarse_v, skip_v, cot_v, upw, convw, upwt, convwt,
    xf, fs, ft, af, gf, dfac, ce, tv, tvp, av, gv, actt, dec_v, gc_v,
    m_up, m_dn, m_lf, m_rt, m_co, r_bot, r_top, r_rt, r_lf, r_co,
    gsum, r0, s1, r1c, r1u, a1c, a1u, s2c, s2u, r2c, r2u, pad, a3, s3, r3,
    in_sem, out_sem, hs, hr, s0s, s0r, s1s, s1r, s2s, s2r, s3s, s3r,
):
    XH, Y, Z, XL = dims
    NX = XH * XL
    HL = CH // XL
    FB = 9 * CH // (XH * Y * 2)
    CB = CH // (Z * XL)
    nface, nband = XH * Y * 2, Z * XL
    face, band = lax.axis_index("face"), lax.axis_index("band")
    core = face % 2
    yy = (face // 2) % Y
    xh = face // (2 * Y)
    xl = band % XL
    zz = band // XL
    xx = xh * XL + xl

    def dev(xx_, yy_, core_, zz_):
        return {
            "face": (xx_ // XL) * (2 * Y) + yy_ * 2 + core_,
            "band": zz_ * XL + xx_ % XL,
        }

    def near(di, dj):
        return {"face": (face + dj + nface) % nface, "band": (band + di + nband) % nband}

    def at_core():
        return dev(xx, yy, 1 - core, zz)

    def at_y(d):
        return dev(xx, (yy + d) % Y, core, zz)

    def at_x(d):
        return dev((xx + d) % NX, yy, core, zz)

    def at_z(d):
        return dev(xx, yy, core, (zz + d) % Z)

    ways = [(-1, 0), (1, 0), (0, -1), (0, 1), (-1, -1), (-1, 1), (1, -1), (1, 1)]
    partners = [near(*w) for w in ways] + [at_core()]
    partners += [at_y(d) for d in range(1, Y)] + [at_x(d) for d in range(1, NX)]
    partners += [at_z(d) for d in range(1, Z)]
    barrier = pltpu.get_barrier_semaphore()
    for p in partners:
        pl.semaphore_signal(barrier, inc=1, device_id=p, device_id_type=MESH)

    loads = [
        pltpu.make_async_copy(src, dst, in_sem.at[n])
        for n, (src, dst) in enumerate(
            ((coarse_h, coarse_v), (skip_h, skip_v), (cot_h, cot_v), (convw_h, convw), (upw_h, upw))
        )
    ]
    for c in loads:
        c.start()

    def rows(a, i, col, n):
        return ld(xf, a * AREA + (i + 2) * XC + 8 + col, n, XC)

    for c in loads[:3]:
        c.wait()

    def spread(i, carry):
        base = pl.multiple_of((i + 2) * XC + 8, 8)
        st(xf, base, CJ, coarse_v[i].astype(F32))
        for src, stage, first in ((skip_v, fs, 1), (cot_v, ft, 5)):
            for r in range(2):
                st(stage, r * 2 * CJ, 2 * CJ, src[2 * i + r].astype(F32))
            for r in range(2):
                for s in range(2):
                    part = ld(stage, r * 2 * CJ + s, CJ, 2)
                    st(xf, pl.multiple_of(base + (first + 2 * r + s) * AREA, 8), CJ, part)
        return carry

    lax.fori_loop(0, RI, spread, 0)

    for n, a in enumerate(MSG_UP):
        m_up[n] = ld(xf, a * AREA + 2 * XC + 8, CJ).astype(BF16)
    for n, a in enumerate(MSG_DOWN):
        m_dn[n] = ld(xf, a * AREA + (RI + 1) * XC + 8, CJ).astype(BF16)
    for n, a in enumerate(MSG_LEFT):
        m_lf[n] = rows(a, 0, 0, 16).astype(BF16)
    for n, a in enumerate(MSG_RIGHT):
        m_rt[n] = rows(a, 0, CJ - 1, 16).astype(BF16)
    for m, (di, dj, fields) in enumerate(CORNERS):
        for n, a in enumerate(fields):
            at = a * AREA + (2 + (0 if di < 0 else RI - 1)) * XC + 8 + (0 if dj < 0 else CJ - 1)
            m_co[m, n : n + 1] = ld(xf, at, 1)

    pl.semaphore_wait(barrier, len(partners))

    def remote(src, dst, ssem, rsem, to):
        return pltpu.make_async_remote_copy(
            src_ref=src, dst_ref=dst, send_sem=ssem, recv_sem=rsem, device_id=to, device_id_type=MESH
        )

    halo = [
        remote(m_up, r_bot, hs.at[0], hr.at[0], near(-1, 0)),
        remote(m_dn, r_top, hs.at[1], hr.at[1], near(1, 0)),
        remote(m_lf, r_rt, hs.at[2], hr.at[2], near(0, -1)),
        remote(m_rt, r_lf, hs.at[3], hr.at[3], near(0, 1)),
    ]
    for m, (di, dj, _) in enumerate(CORNERS):
        halo.append(remote(m_co.at[m], r_co.at[m], hs.at[4 + m], hr.at[4 + m], near(di, dj)))
    for c in halo:
        c.start()

    for c in loads[3:]:
        c.wait()

    def turn(t, carry):
        at = pl.multiple_of(t * CH, CH)
        convwt[pl.ds(at, CH), :] = convw[pl.ds(at, CH), :].T
        upwt[pl.ds(at, CH), :] = upw[pl.ds(at, CH), :].T
        return carry

    lax.fori_loop(0, 9, turn, 0)
    src = lax.broadcasted_iota(jnp.int32, (CH, CH), 0)
    dst = lax.broadcasted_iota(jnp.int32, (CH, CH), 1)
    wanted = (((dst % HL) // CB) * XL + dst // HL) * CB + dst % CB
    perm = jnp.where(src == wanted, 1.0, 0.0).astype(BF16)

    for c in halo:
        c.wait()
    keep_top = jnp.where(band == 0, 0.0, 1.0)
    keep_bot = jnp.where(band == nband - 1, 0.0, 1.0)
    for n, a in enumerate(MSG_UP):
        st(xf, a * AREA + (RI + 2) * XC + 8, CJ, r_bot[n].astype(F32) * keep_bot)
    for n, a in enumerate(MSG_DOWN):
        st(xf, a * AREA + XC + 8, CJ, r_top[n].astype(F32) * keep_top)
    for n, a in enumerate(MSG_LEFT):
        st(xf, a * AREA + 2 * XC + 8 + CJ, RI, r_rt[n].astype(F32)[:RI], XC)
    for n, a in enumerate(MSG_RIGHT):
        st(xf, a * AREA + 2 * XC + 7, RI, r_lf[n].astype(F32)[:RI], XC)
    for m, (di, dj, fields) in enumerate(CORNERS):
        keep = keep_bot if di < 0 else keep_top
        for n, a in enumerate(fields):
            at = a * AREA + (RI + 2 if di < 0 else 1) * XC + (8 + CJ if dj < 0 else 7)
            st(xf, at, 1, r_co[m, n : n + 1] * keep)

    def window(ref, a, i, dj, n):
        return jnp.concatenate(
            [ld(ref, a * AREA + (i + q + 2) * XC + 8 + dj, CJ) for q in range(n)], axis=0
        )

    for di in range(2):
        for dj in range(2):
            ce[2 * di + dj, :224] = window(xf, 0, di - 1, dj, 14).astype(BF16)
            ce[2 * di + dj, 224:240] = rows(0, di - 1, dj - 1, 16).astype(BF16)
            ce[2 * di + dj, 240:] = rows(0, di - 1, CJ, 16).astype(BF16)
    line = lax.broadcasted_iota(jnp.int32, (CH, CH), 0)
    cell_row = jnp.where(line < 224, line // 16, line % 16)
    ghost = ((band == 0) & (cell_row == 0)) | ((band == nband - 1) & (cell_row == 13))
    for r in range(2):
        for s in range(2):
            ph = 2 * r + s
            total = None
            for k, di in ((1, 0),) if r == 0 else ((2, 0), (0, 1)):
                for l, dj in ((1, 0),) if s == 0 else ((2, 0), (0, 1)):
                    term = dot(ce[2 * di + dj], upw[(3 * k + l) * CH : (3 * k + l + 1) * CH, :])
                    total = term if total is None else total + term
            skip_e = jnp.concatenate(
                [window(xf, 1 + ph, -1, 0, 14), rows(1 + ph, -1, -1, 16), rows(1 + ph, -1, CJ, 16)], axis=0
            )
            pre = total + skip_e
            sig = jax.nn.sigmoid(pre)
            act = jnp.where(ghost, 0.0, pre * sig).astype(BF16).astype(F32)
            dfac[ph] = jnp.where(ghost, 0.0, sig * (1.0 + pre * (1.0 - sig)))
            for q in range(14):
                st(af, ph * AREA + (q + 1) * XC + 8, CJ, act[16 * q : 16 * q + 16])
            st(af, ph * AREA + XC + 7, 16, act[224:240], XC)
            st(af, ph * AREA + XC + 8 + CJ, 16, act[240:], XC)
            actt[:, ph * 192 : ph * 192 + 192] = act[16:208].T.astype(BF16)

    for r in range(2):
        for s in range(2):
            for v, dj in enumerate((0, 1 if s == 0 else -1)):
                n = (2 * r + s) * 2 + v
                tv[n] = window(xf, 5 + 2 * r + s, -1, dj, 14).astype(BF16)
                tvp[n] = dot(tv[n], perm).astype(BF16)

    def view(ref, er, es, i0, n):
        (r, di), (s, dj) = split(er), split(es)
        at = (i0 + di + 1) * 16
        return ref[(2 * r + s) * 2 + (1 if dj else 0), at : at + 16 * n]

    def put(arr, t, value):
        start = t * CH
        while start < (t + 1) * CH:
            f, off = divmod(start, FB)
            stop = min((t + 1) * CH, (f + 1) * FB)
            gsum[arr, f // (2 * Y), (f // 2) % Y, f % 2, off : off + stop - start] = value[
                start - t * CH : stop - t * CH
            ]
            start = stop

    for t, (k, l) in enumerate(TAPS):
        right = jnp.concatenate(
            [view(tvp, r - k + 1, s - l + 1, 0, RI) for r in range(2) for s in range(2)], axis=0
        )
        put(0, t, dot(actt[...], right).astype(BF16))

    def first(arr):
        return remote(
            gsum.at[arr, :, :, 1 - core], r0.at[arr], s0s.at[arr], s0r.at[arr], at_core()
        )

    def second(arr):
        def add(n, carry):
            a, b = n // Y, n % Y
            total = gsum[arr, a, b, core].astype(F32) + r0[arr, a, b].astype(F32)
            s1[arr, a, b] = total.astype(BF16)
            return carry

        lax.fori_loop(0, XH * Y, add, 0)

    step0c = first(0)
    step0c.start()

    for r in range(2):
        for s in range(2):
            ph = 2 * r + s
            i0 = -1 if r else 0
            n = RI - i0
            left = jnp.concatenate([view(tv, r - k + 1, s - l + 1, i0, n) for k, l in TAPS], axis=1)
            if s:
                column = []
                for k, l in TAPS:
                    (r2, di), (s2, dj) = split(r - k + 1), split(s - l + 1)
                    column.append(rows(5 + 2 * r2 + s2, -1 + di, -1 + dj, 16).astype(BF16))
                left = jnp.concatenate([left, jnp.concatenate(column, axis=1)], axis=0)
            grad = dot(left, convwt[...])
            main = (grad[: 16 * n] * dfac[ph, (i0 + 1) * 16 : 208]).astype(BF16).astype(F32)
            for q in range(n):
                st(gf, ph * AREA + (i0 + q + 2) * XC + 8, CJ, main[16 * q : 16 * q + 16])
            if s:
                side = (grad[16 * n :] * dfac[ph, 224:240]).astype(BF16).astype(F32)
                st(gf, ph * AREA + XC + 7, 16, side, XC)

    step0c.wait()
    second(0)
    step1c = [
        remote(s1.at[0, :, (yy + d) % Y], r1c.at[Y - d - 1], s1s.at[0, d - 1], s1r.at[0, Y - d - 1], at_y(d))
        for d in range(1, Y)
    ]
    for c in step1c:
        c.start()

    coarse_t = window(xf, 0, 0, 0, RI).T.astype(BF16)
    for t, (k, l) in enumerate(TAPS):
        (r, di), (s, dj) = split(k - 1), split(l - 1)
        part = window(gf, 2 * r + s, di, dj, RI).astype(BF16)
        gv[:, t * CH : (t + 1) * CH] = part
        put(1, t, dot(coarse_t, dot(part, perm).astype(BF16)).astype(BF16))

    step0u = first(1)
    step0u.start()

    for r in range(2):
        for s in range(2):
            for v, dj in enumerate((0, 1 if s == 0 else -1)):
                av[(2 * r + s) * 2 + v] = window(af, 2 * r + s, -1, dj, 14).astype(BF16)

    step0u.wait()
    second(1)

    def x_piece(ref, d):
        x2 = (xx + d) % NX
        return ref.at[x2 // XL, :, :, pl.ds(pl.multiple_of((x2 % XL) * HL, HL), HL)]

    step1u = [
        remote(x_piece(s1.at[1], d), r1u.at[NX - d - 1], s1s.at[1, d - 1], s1r.at[1, NX - d - 1], at_x(d))
        for d in range(1, NX)
    ]
    for c in step1u:
        c.start()

    def decode(r, s):
        left = jnp.concatenate([view(av, r + k - 1, s + l - 1, 0, RI) for k, l in TAPS], axis=1)
        out = dot(left, convw[...])
        for i in range(RI):
            st(dec_v, (2 * i + r) * 2 * CJ + s, CJ, out[16 * i : 16 * i + 16], 2)

    decode(0, 0)
    decode(0, 1)

    for c in step1c:
        c.wait()
    for a in range(XH):
        total = gsum[0, a, yy, core].astype(F32) + r0[0, a, yy].astype(F32)
        for d in range(Y - 1):
            total = total + r1c[d, a].astype(F32)
        a1c[a] = total
        s2c[a] = total.astype(BF16)

    def x_piece2(ref, d):
        x2 = (xx + d) % NX
        return ref.at[x2 // XL, :, pl.ds(pl.multiple_of((x2 % XL) * HL, HL), HL)]

    step2c = [
        remote(x_piece2(s2c, d), r2c.at[NX - d - 1], s2s.at[0, d - 1], s2r.at[0, NX - d - 1], at_x(d))
        for d in range(1, NX)
    ]
    for c in step2c:
        c.start()

    decode(1, 0)
    decode(1, 1)

    own = pl.ds(pl.multiple_of(xl * HL, HL), HL)
    for c in step1u:
        c.wait()
    for b in range(Y):
        total = gsum[1, xh, b, core, :, own].astype(F32) + r0[1, xh, b, :, own].astype(F32)
        for d in range(NX - 1):
            total = total + r1u[d, b].astype(F32)
        a1u[b] = total
        s2u[b] = total.astype(BF16)
    step2u = [
        remote(s2u.at[(yy + d) % Y], r2u.at[Y - d - 1], s2s.at[1, d - 1], s2r.at[1, Y - d - 1], at_y(d))
        for d in range(1, Y)
    ]
    for c in step2u:
        c.start()

    def third(arr, total):
        pad[arr, :FB] = total
        turned = pad[arr].T
        for z in range(Z):
            a3[arr, z] = turned[z * CB : (z + 1) * CB]
            s3[arr, z] = turned[z * CB : (z + 1) * CB].astype(BF16)
        steps = [
            remote(s3.at[arr, (zz + d) % Z], r3.at[arr, Z - d - 1], s3s.at[arr, d - 1], s3r.at[arr, Z - d - 1], at_z(d))
            for d in range(1, Z)
        ]
        for c in steps:
            c.start()
        return steps

    for c in step2c:
        c.wait()
    total = a1c[xh, :, own]
    for d in range(NX - 1):
        total = total + r2c[d].astype(F32)
    step3c = third(0, total)

    gc_v[...] = dot(gv[...], upwt[...]).astype(BF16)
    gc_copy = pltpu.make_async_copy(gc_v, gc_h, out_sem.at[0])
    gc_copy.start()
    for p in range(2 * RI):
        skip_v[p] = ld(dec_v, p * 2 * CJ, 2 * CJ).astype(BF16)
    dec_copy = pltpu.make_async_copy(skip_v, dec_h, out_sem.at[1])
    dec_copy.start()

    for c in step2u:
        c.wait()
    total = a1u[yy]
    for d in range(Y - 1):
        total = total + r2u[d].astype(F32)
    step3u = third(1, total)

    for arr, steps, out in ((0, step3c, gw_o), (1, step3u, gu_o)):
        for c in steps:
            c.wait()
        total = a3[arr, zz]
        for d in range(Z - 1):
            total = total + r3[arr, d].astype(F32)
        out[...] = total
    gc_copy.wait()
    dec_copy.wait()


def local(dims, coarse, skip, up_weight, conv_weight, cotangent):
    XH, Y, Z, XL = dims
    NX, HL = XH * XL, CH // XL
    FB, CB = 9 * CH // (XH * Y * 2), CH // (Z * XL)
    FP = -(-FB // 128) * 128
    any_, vmem = pl.BlockSpec(memory_space=pl.ANY), pl.BlockSpec(memory_space=pltpu.VMEM)
    V, dma = pltpu.VMEM, pltpu.SemaphoreType.DMA
    scratch = [
        V((RI, CJ, CH), BF16), V((2 * RI, 2 * CJ, CH), BF16), V((2 * RI, 2 * CJ, CH), BF16),
        V((9 * CH, CH), BF16), V((9 * CH, CH), BF16), V((9 * CH, CH), BF16), V((9 * CH, CH), BF16),
        V((2, 9 * AREA, 128), F32), V((2, 4 * CJ, 128), F32), V((2, 4 * CJ, 128), F32),
        V((2, 4 * AREA, 128), F32), V((2, 4 * AREA, 128), F32), V((4, CH, CH), F32),
        V((4, CH, CH), BF16), V((8, 224, CH), BF16), V((8, 224, CH), BF16), V((8, 224, CH), BF16),
        V((192, 9 * CH), BF16), V((CH, 768), BF16), V((2, 4 * RI * CJ, 128), F32), V((192, CH), BF16),
        V((5, 16, CH), BF16), V((7, 16, CH), BF16), V((5, 16, CH), BF16), V((7, 16, CH), BF16), V((4, 8, CH), F32),
        V((5, 16, CH), BF16), V((7, 16, CH), BF16), V((5, 16, CH), BF16), V((7, 16, CH), BF16), V((4, 8, CH), F32),
        V((2, XH, Y, 2, FB, CH), BF16), V((2, XH, Y, FB, CH), BF16), V((2, XH, Y, FB, CH), BF16),
        V((Y - 1, XH, FB, CH), BF16), V((NX - 1, Y, FB, HL), BF16),
        V((XH, FB, CH), F32), V((Y, FB, HL), F32), V((XH, FB, CH), BF16), V((Y, FB, HL), BF16),
        V((NX - 1, FB, HL), BF16), V((Y - 1, FB, HL), BF16),
        V((2, FP, HL), F32), V((2, Z, CB, FP), F32), V((2, Z, CB, FP), BF16), V((2, Z - 1, CB, FP), BF16),
        dma((5,)), dma((2,)), dma((8,)), dma((8,)), dma((2,)), dma((2,)),
        dma((2, 3)), dma((2, 3)), dma((2, 3)), dma((2, 3)), dma((2, Z - 1)), dma((2, Z - 1)),
    ]
    decoded, grad_coarse, grad_up, grad_conv = pl.pallas_call(
        functools.partial(kernel, dims),
        out_shape=(
            jax.ShapeDtypeStruct((2 * RI, 2 * CJ, CH), BF16),
            jax.ShapeDtypeStruct((RI * CJ, CH), BF16),
            jax.ShapeDtypeStruct((CB, FP), F32),
            jax.ShapeDtypeStruct((CB, FP), F32),
        ),
        in_specs=[any_] * 5,
        out_specs=(any_, any_, vmem, vmem),
        scratch_shapes=scratch,
        compiler_params=pltpu.CompilerParams(
            collective_id=0, has_side_effects=True, vmem_limit_bytes=60 * 2**20
        ),
    )(coarse, skip, up_weight.reshape(9 * CH, CH), conv_weight.reshape(9 * CH, CH), cotangent)
    return (
        decoded,
        grad_coarse.reshape(RI, CJ, CH),
        grad_up[:, :FB].T,
        grad_conv[:, :FB].T,
    )


def build(mesh, dims):
    cells = P("band", "face", None)
    return jax.shard_map(
        functools.partial(local, dims),
        mesh=mesh,
        in_specs=(cells, cells, P(), P(), cells),
        out_specs=(cells, cells, P("face", "band"), P("face", "band")),
        check_vma=False,
    )


def solution(mesh):
    return build(mesh, (2, 4, 8, 2))
```

```python
import functools

import jax
import jax.numpy as jnp
from jax import lax
from jax.experimental import pallas as pl
from jax.experimental.pallas import tpu as pltpu
from jax.sharding import PartitionSpec as P

F32, BF16 = jnp.float32, jnp.bfloat16
MESH = pl.DeviceIdType.MESH
CH = 256
RI, CJ = 12, 16
XR, XC = 18, 32
AREA = XR * XC

UP1, UP2 = (0, 5, 6), (1, 2)
DOWN1, DOWN2 = (7, 8), (0, 3, 4, 5, 6)
LEFT1, LEFT2 = (0, 5, 7), (1, 3)
RIGHT1, RIGHT2 = (6, 8), (0, 2, 4, 5, 7)
CORNERS = (
    (-1, -1, (0, 1, 5)),
    (-1, 1, (0, 2, 5, 6)),
    (1, -1, (0, 3, 5, 7)),
    (1, 1, (0, 4, 5, 6, 7, 8)),
)
TAPS = [(k, l) for k in range(3) for l in range(3)]


def split(e):
    return e % 2, e // 2


def dot(a, b):
    return jnp.dot(a, b, preferred_element_type=F32)


def ld(ref, at, n, stride=1):
    if stride == 1:
        return jnp.concatenate([ref[h, pl.ds(at, n), :] for h in range(2)], axis=-1)
    return jnp.concatenate([ref[h, pl.ds(at, n, stride=stride), :] for h in range(2)], axis=-1)


def st(ref, at, n, value, stride=1):
    for h in range(2):
        part = value[:, 128 * h : 128 * h + 128]
        if stride == 1:
            ref[h, pl.ds(at, n), :] = part
        else:
            ref[h, pl.ds(at, n, stride=stride), :] = part


def kernel(
    dims,
    coarse_h, skip_h, upw_h, convw_h, cot_h,
    dec_o, gc_o, gu_o, gw_o,
    coarse_v, skip_v, cot_v, upw, convw, upwt, convwt,
    xf, fs, ft, af, gf, dfac, dghost, ce, cg, tv, tvp, av, gv, actt, dec_v,
    m_1, m_2, m_co, r_1, r_2, r_co,
    gsum, r0, s1, r1a, r1b, a1a, a1b, s2a, s2b, r2a, r2b, pad, a3, s3, r3,
    in_sem, hs, hr, s0s, s0r, s1s, s1r, s2s, s2r, s3s, s3r,
):
    loads = [
        pltpu.make_async_copy(src, dst, in_sem.at[n])
        for n, (src, dst) in enumerate(
            ((coarse_h, coarse_v), (cot_h, cot_v), (skip_h, skip_v), (convw_h, convw), (upw_h, upw))
        )
    ]
    for c in loads:
        c.start()

    XH, Y, Z, XL = dims
    NX = XH * XL
    HL = CH // XL
    FB = 9 * CH // (XH * Y * 2)
    RA = FB // 16 * 5 // 9 * 16
    CB = CH // (Z * XL)
    nface, nband = XH * Y * 2, Z * XL
    face, band = lax.axis_index("face"), lax.axis_index("band")
    core = face % 2
    yy = (face // 2) % Y
    xh = face // (2 * Y)
    xl = band % XL
    zz = band // XL
    xx = xh * XL + xl

    def dev(xx_, yy_, core_, zz_):
        return {
            "face": (xx_ // XL) * (2 * Y) + yy_ * 2 + core_,
            "band": zz_ * XL + xx_ % XL,
        }

    def near(di, dj):
        return {"face": (face + dj + nface) % nface, "band": (band + di + nband) % nband}

    def at_core():
        return dev(xx, yy, 1 - core, zz)

    def at_y(d):
        return dev(xx, (yy + d) % Y, core, zz)

    def at_x(d):
        return dev((xx + d) % NX, yy, core, zz)

    def at_z(d):
        return dev(xx, yy, core, (zz + d) % Z)

    ways = [(-1, 0), (1, 0), (0, -1), (0, 1), (-1, -1), (-1, 1), (1, -1), (1, 1)]
    partners = [near(*w) for w in ways] + [at_core()]
    partners += [at_y(d) for d in range(1, Y)] + [at_x(d) for d in range(1, NX)]
    partners += [at_z(d) for d in range(1, Z)]
    barrier = pltpu.get_barrier_semaphore()
    for p in partners:
        pl.semaphore_signal(barrier, inc=1, device_id=p, device_id_type=MESH)

    def rows(a, i, col, n):
        return ld(xf, a * AREA + (i + 2) * XC + 8 + col, n, XC)

    for c in loads[:3]:
        c.wait()

    def spread(i, carry):
        base = pl.multiple_of((i + 2) * XC + 8, 8)
        st(xf, base, CJ, coarse_v[i].astype(F32))
        for src, stage, first in ((skip_v, fs, 1), (cot_v, ft, 5)):
            for r in range(2):
                st(stage, r * 2 * CJ, 2 * CJ, src[2 * i + r].astype(F32))
            for r in range(2):
                for s in range(2):
                    part = ld(stage, r * 2 * CJ + s, CJ, 2)
                    st(xf, pl.multiple_of(base + (first + 2 * r + s) * AREA, 8), CJ, part)
        return carry

    lax.fori_loop(0, RI, spread, 0)

    def message(buf, fields, way):
        for n, a in enumerate(fields):
            if way < 2:
                buf[way, n] = ld(xf, a * AREA + (2 if way == 0 else RI + 1) * XC + 8, CJ).astype(BF16)
            else:
                buf[way, n] = rows(a, 0, 0 if way == 2 else CJ - 1, 16).astype(BF16)

    for way, fields in enumerate((UP1, DOWN1, LEFT1, RIGHT1)):
        message(m_1, fields, way)
    for m, (di, dj, fields) in enumerate(CORNERS):
        for n, a in enumerate(fields):
            at = a * AREA + (2 + (0 if di < 0 else RI - 1)) * XC + 8 + (0 if dj < 0 else CJ - 1)
            m_co[m, n : n + 1] = ld(xf, at, 1)

    pl.semaphore_wait(barrier, len(partners))

    def remote(src, dst, ssem, rsem, to):
        return pltpu.make_async_remote_copy(
            src_ref=src, dst_ref=dst, send_sem=ssem, recv_sem=rsem, device_id=to, device_id_type=MESH
        )

    halo1, halo2 = [], []
    for m, (di, dj, _) in enumerate(CORNERS):
        halo1.append(remote(m_co.at[m], r_co.at[m], hs.at[m], hr.at[m], near(di, dj)))
    for way, fields in enumerate((UP1, DOWN1, LEFT1, RIGHT1)):
        n = len(fields)
        halo1.append(
            remote(m_1.at[way, :n], r_1.at[way, :n], hs.at[4 + way], hr.at[4 + way], near(*ways[way]))
        )
    for c in halo1:
        c.start()
    for way, fields in enumerate((UP2, DOWN2, LEFT2, RIGHT2)):
        message(m_2, fields, way)
        n = len(fields)
        halo2.append(
            remote(m_2.at[way, :n], r_2.at[way, :n], hs.at[8 + way], hr.at[8 + way], near(*ways[way]))
        )
    for c in halo2:
        c.start()

    for c in loads[3:]:
        c.wait()

    def turn(t, carry):
        at = pl.multiple_of(t * CH, CH)
        convwt[pl.ds(at, CH), :] = convw[pl.ds(at, CH), :].T
        upwt[pl.ds(at, CH), :] = upw[pl.ds(at, CH), :].T
        return carry

    lax.fori_loop(0, 9, turn, 0)
    src = lax.broadcasted_iota(jnp.int32, (CH, CH), 0)
    dst = lax.broadcasted_iota(jnp.int32, (CH, CH), 1)
    wanted = (((dst % HL) // CB) * XL + dst // HL) * CB + dst % CB
    perm = jnp.where(src == wanted, 1.0, 0.0).astype(BF16)

    keep_top = jnp.where(band == 0, 0.0, 1.0)
    keep_bot = jnp.where(band == nband - 1, 0.0, 1.0)

    def receive(buf, fields, way):
        for n, a in enumerate(fields):
            value = buf[way, n].astype(F32)
            if way == 0:
                st(xf, a * AREA + (RI + 2) * XC + 8, CJ, value * keep_bot)
            elif way == 1:
                st(xf, a * AREA + XC + 8, CJ, value * keep_top)
            else:
                st(xf, a * AREA + 2 * XC + (8 + CJ if way == 2 else 7), RI, value[:RI], XC)

    for c in halo1:
        c.wait()
    for way, fields in enumerate((UP1, DOWN1, LEFT1, RIGHT1)):
        receive(r_1, fields, way)
    for m, (di, dj, fields) in enumerate(CORNERS):
        keep = keep_bot if di < 0 else keep_top
        for n, a in enumerate(fields):
            at = a * AREA + (RI + 2 if di < 0 else 1) * XC + (8 + CJ if dj < 0 else 7)
            st(xf, at, 1, r_co[m, n : n + 1] * keep)

    def window(ref, a, i, dj, n):
        return jnp.concatenate(
            [ld(ref, a * AREA + (i + q + 2) * XC + 8 + dj, CJ) for q in range(n)], axis=0
        )

    def up(left, r, s):
        total = None
        for k, di in ((1, 0),) if r == 0 else ((2, 0), (0, 1)):
            for l, dj in ((1, 0),) if s == 0 else ((2, 0), (0, 1)):
                term = dot(left[2 * di + dj], upw[(3 * k + l) * CH : (3 * k + l + 1) * CH, :])
                total = term if total is None else total + term
        return total

    for di in range(2):
        for dj in range(2):
            ce[2 * di + dj] = window(xf, 0, di, dj, RI).astype(BF16)
    for r in range(2):
        for s in range(2):
            ph = 2 * r + s
            pre = up(ce, r, s) + window(xf, 1 + ph, 0, 0, RI)
            sig = jax.nn.sigmoid(pre)
            act = (pre * sig).astype(BF16).astype(F32)
            dfac[ph] = sig * (1.0 + pre * (1.0 - sig))
            for q in range(RI):
                st(af, ph * AREA + (q + 2) * XC + 8, CJ, act[16 * q : 16 * q + 16])
            actt[:, ph * 192 : ph * 192 + 192] = act.T.astype(BF16)

    for r in range(2):
        for s in range(2):
            for v, dj in enumerate((0, 1 if s == 0 else -1)):
                n = (2 * r + s) * 2 + v
                tv[n] = window(xf, 5 + 2 * r + s, -1, dj, 14).astype(BF16)
                tvp[n] = dot(tv[n], perm).astype(BF16)

    def view(ref, er, es, i0, n):
        (r, di), (s, dj) = split(er), split(es)
        at = (i0 + di + 1) * 16
        return ref[(2 * r + s) * 2 + (1 if dj else 0), at : at + 16 * n]

    def put(arr, t, value):
        start = t * CH
        while start < (t + 1) * CH:
            f, off = divmod(start, FB)
            stop = min((t + 1) * CH, (f + 1) * FB)
            gsum[arr, f // (2 * Y), (f // 2) % Y, f % 2, off : off + stop - start] = value[
                start - t * CH : stop - t * CH
            ]
            start = stop

    for t, (k, l) in enumerate(TAPS):
        right = jnp.concatenate(
            [view(tvp, r - k + 1, s - l + 1, 0, RI) for r in range(2) for s in range(2)], axis=0
        )
        put(0, t, dot(actt[...], right).astype(BF16))

    def first(arr):
        return remote(
            gsum.at[arr, :, :, 1 - core], r0.at[arr], s0s.at[arr], s0r.at[arr], at_core()
        )

    def second(arr):
        def add(n, carry):
            a, b = n // Y, n % Y
            total = gsum[arr, a, b, core].astype(F32) + r0[arr, a, b].astype(F32)
            s1[arr, a, b] = total.astype(BF16)
            return carry

        lax.fori_loop(0, XH * Y, add, 0)

    step0c = first(0)
    step0c.start()

    for c in halo2:
        c.wait()
    for way, fields in enumerate((UP2, DOWN2, LEFT2, RIGHT2)):
        receive(r_2, fields, way)

    def border(a, di, dj):
        return jnp.concatenate(
            [window(xf, a, di - 1, dj, 1), window(xf, a, di + RI, dj, 1)]
            + [rows(a, di - 1, dj - 1, 16), rows(a, di - 1, dj + CJ, 16)],
            axis=0,
        )

    for di in range(2):
        for dj in range(2):
            cg[2 * di + dj] = border(0, di, dj).astype(BF16)
    line = lax.broadcasted_iota(jnp.int32, (64, CH), 0)
    first_row = (line < 16) | ((line >= 32) & (line % 16 == 0))
    last_row = ((line >= 16) & (line < 32)) | ((line >= 32) & (line % 16 == RI + 1))
    ghost = ((band == 0) & first_row) | ((band == nband - 1) & last_row)
    for r in range(2):
        for s in range(2):
            ph = 2 * r + s
            pre = up(cg, r, s) + border(1 + ph, 0, 0)
            sig = jax.nn.sigmoid(pre)
            act = jnp.where(ghost, 0.0, pre * sig).astype(BF16).astype(F32)
            dghost[ph] = jnp.where(ghost, 0.0, sig * (1.0 + pre * (1.0 - sig)))
            st(af, ph * AREA + XC + 8, CJ, act[:16])
            st(af, ph * AREA + (RI + 2) * XC + 8, CJ, act[16:32])
            st(af, ph * AREA + XC + 7, 16, act[32:48], XC)
            st(af, ph * AREA + XC + 8 + CJ, 16, act[48:], XC)

    for s in range(2):
        for v, dj in enumerate((0, 1 if s == 0 else -1)):
            tv[2 * s + v, :16] = window(xf, 5 + s, -1, dj, 1).astype(BF16)

    for r in range(2):
        for s in range(2):
            ph = 2 * r + s
            i0 = -1 if r else 0
            n = RI - i0
            left = jnp.concatenate([view(tv, r - k + 1, s - l + 1, i0, n) for k, l in TAPS], axis=1)
            if s:
                column = []
                for k, l in TAPS:
                    (r2, di), (s2, dj) = split(r - k + 1), split(s - l + 1)
                    column.append(rows(5 + 2 * r2 + s2, -1 + di, -1 + dj, 16).astype(BF16))
                left = jnp.concatenate([left, jnp.concatenate(column, axis=1)], axis=0)
            grad = dot(left, convwt[...])
            slope = jnp.concatenate([dghost[ph, :16], dfac[ph]], axis=0) if r else dfac[ph]
            main = (grad[: 16 * n] * slope).astype(BF16).astype(F32)
            for q in range(n):
                st(gf, ph * AREA + (i0 + q + 2) * XC + 8, CJ, main[16 * q : 16 * q + 16])
            if s:
                side = (grad[16 * n :] * dghost[ph, 32:48]).astype(BF16).astype(F32)
                st(gf, ph * AREA + XC + 7, 16, side, XC)

    coarse_t = window(xf, 0, 0, 0, RI).T.astype(BF16)
    for t, (k, l) in enumerate(TAPS):
        (r, di), (s, dj) = split(k - 1), split(l - 1)
        part = window(gf, 2 * r + s, di, dj, RI).astype(BF16)
        gv[:, t * CH : (t + 1) * CH] = part
        put(1, t, dot(coarse_t, dot(part, perm).astype(BF16)).astype(BF16))
    step0u = first(1)
    step0u.start()

    def half(x2):
        return pl.ds(pl.multiple_of((x2 % XL) * HL, HL), HL)

    def stage1(arr):
        steps = [[], []]
        for d in range(1, max(Y, NX)):
            if d < Y:
                q = Y - d - 1
                steps[0].append(
                    remote(
                        s1.at[arr, :, (yy + d) % Y, :RA], r1a.at[arr, q],
                        s1s.at[arr, 0, d - 1], s1r.at[arr, 0, q], at_y(d),
                    )
                )
                steps[0][-1].start()
            if d < NX:
                q, x2 = NX - d - 1, (xx + d) % NX
                steps[1].append(
                    remote(
                        s1.at[arr, x2 // XL, :, RA:, half(x2)], r1b.at[arr, q],
                        s1s.at[arr, 1, d - 1], s1r.at[arr, 1, q], at_x(d),
                    )
                )
                steps[1][-1].start()
        return steps

    def stage2a(arr, steps):
        for c in steps:
            c.wait()
        for a in range(XH):
            total = gsum[arr, a, yy, core, :RA].astype(F32) + r0[arr, a, yy, :RA].astype(F32)
            for d in range(Y - 1):
                total = total + r1a[arr, d, a].astype(F32)
            a1a[arr, a] = total
            s2a[arr, a] = total.astype(BF16)
        out = []
        for d in range(1, NX):
            q, x2 = NX - d - 1, (xx + d) % NX
            out.append(
                remote(
                    s2a.at[arr, x2 // XL, :, half(x2)], r2a.at[arr, q],
                    s2s.at[arr, 0, d - 1], s2r.at[arr, 0, q], at_x(d),
                )
            )
            out[-1].start()
        return out

    def stage2b(arr, steps):
        for c in steps:
            c.wait()
        own = half(xx)
        for b in range(Y):
            total = gsum[arr, xh, b, core, RA:, own].astype(F32) + r0[arr, xh, b, RA:, own].astype(F32)
            for d in range(NX - 1):
                total = total + r1b[arr, d, b].astype(F32)
            a1b[arr, b] = total
            s2b[arr, b] = total.astype(BF16)
        out = []
        for d in range(1, Y):
            q = Y - d - 1
            out.append(
                remote(
                    s2b.at[arr, (yy + d) % Y], r2b.at[arr, q],
                    s2s.at[arr, 1, d - 1], s2r.at[arr, 1, q], at_y(d),
                )
            )
            out[-1].start()
        return out

    def stage3(arr, steps):
        for c in steps[0]:
            c.wait()
        total = a1a[arr, xh, :, half(xx)]
        for d in range(NX - 1):
            total = total + r2a[arr, d].astype(F32)
        pad[arr, :RA] = total
        for c in steps[1]:
            c.wait()
        total = a1b[arr, yy]
        for d in range(Y - 1):
            total = total + r2b[arr, d].astype(F32)
        pad[arr, RA:FB] = total
        turned = pad[arr].T
        for z in range(Z):
            a3[arr, z] = turned[z * CB : (z + 1) * CB]
            s3[arr, z] = turned[z * CB : (z + 1) * CB].astype(BF16)
        out = []
        for d in range(1, Z):
            q = Z - d - 1
            out.append(
                remote(s3.at[arr, (zz + d) % Z], r3.at[arr, q], s3s.at[arr, d - 1], s3r.at[arr, q], at_z(d))
            )
            out[-1].start()
        return out

    def finish(arr, steps, out):
        for c in steps:
            c.wait()
        total = a3[arr, zz]
        for d in range(Z - 1):
            total = total + r3[arr, d].astype(F32)
        out[...] = total[:, :FB]

    def decode(r, s):
        left = jnp.concatenate([view(av, r + k - 1, s + l - 1, 0, RI) for k, l in TAPS], axis=1)
        out = dot(left, convw[...])
        for i in range(RI):
            st(dec_v, (2 * i + r) * 2 * CJ + s, CJ, out[16 * i : 16 * i + 16], 2)

    step0c.wait()
    second(0)
    step1c = stage1(0)

    for r in range(2):
        for s in range(2):
            for v, dj in enumerate((0, 1 if s == 0 else -1)):
                av[(2 * r + s) * 2 + v] = window(af, 2 * r + s, -1, dj, 14).astype(BF16)

    step0u.wait()
    second(1)
    step1u = stage1(1)

    decode(0, 0)
    decode(0, 1)
    step2c = [stage2a(0, step1c[0]), stage2b(0, step1c[1])]
    decode(1, 0)
    decode(1, 1)
    step3c = stage3(0, step2c)
    gc_o[...] = dot(gv[...], upwt[...]).astype(BF16)
    for p in range(2 * RI):
        dec_o[p] = ld(dec_v, p * 2 * CJ, 2 * CJ).astype(BF16)
    step2u = [stage2a(1, step1u[0]), stage2b(1, step1u[1])]
    step3u = stage3(1, step2u)
    finish(0, step3c, gw_o)
    finish(1, step3u, gu_o)


def deliver(*refs):
    n = (len(refs) - 1) // 2
    copies = [pltpu.make_async_copy(refs[i], refs[n + i], refs[-1].at[i]) for i in range(n)]
    for c in copies:
        c.start()
    for c in copies:
        c.wait()


def local(dims, coarse, skip, up_weight, conv_weight, cotangent):
    XH, Y, Z, XL = dims
    NX, HL = XH * XL, CH // XL
    FB, CB = 9 * CH // (XH * Y * 2), CH // (Z * XL)
    RA = FB // 16 * 5 // 9 * 16
    RB = FB - RA
    FP = -(-FB // 128) * 128
    hbm, vmem = pl.BlockSpec(memory_space=pltpu.HBM), pl.BlockSpec(memory_space=pltpu.VMEM)
    V, dma = pltpu.VMEM, pltpu.SemaphoreType.DMA
    wide = V((9 * CH, CH), BF16)
    scratch = [
        V((RI, CJ, CH), BF16), V((2 * RI, 2 * CJ, CH), BF16), V((2 * RI, 2 * CJ, CH), BF16),
        wide, wide, wide, wide,
        V((2, 9 * AREA, 128), F32), V((2, 4 * CJ, 128), F32), V((2, 4 * CJ, 128), F32),
        V((2, 4 * AREA, 128), F32), V((2, 4 * AREA, 128), F32), V((4, 192, CH), F32), V((4, 64, CH), F32),
        V((4, 192, CH), BF16), V((4, 64, CH), BF16),
        V((8, 224, CH), BF16), V((8, 224, CH), BF16), V((8, 224, CH), BF16),
        V((192, 9 * CH), BF16), V((CH, 768), BF16), V((2, 4 * RI * CJ, 128), F32),
        V((4, 3, 16, CH), BF16), V((4, 5, 16, CH), BF16), V((4, 8, CH), F32),
        V((4, 3, 16, CH), BF16), V((4, 5, 16, CH), BF16), V((4, 8, CH), F32),
        V((2, XH, Y, 2, FB, CH), BF16), V((2, XH, Y, FB, CH), BF16), V((2, XH, Y, FB, CH), BF16),
        V((2, Y - 1, XH, RA, CH), BF16), V((2, NX - 1, Y, RB, HL), BF16),
        V((2, XH, RA, CH), F32), V((2, Y, RB, HL), F32), V((2, XH, RA, CH), BF16), V((2, Y, RB, HL), BF16),
        V((2, NX - 1, RA, HL), BF16), V((2, Y - 1, RB, HL), BF16),
        V((2, FP, HL), F32), V((2, Z, CB, FP), F32), V((2, Z, CB, FP), BF16), V((2, Z - 1, CB, FP), BF16),
        dma((5,)), dma((12,)), dma((12,)), dma((2,)), dma((2,)),
        dma((2, 2, 3)), dma((2, 2, 3)), dma((2, 2, 3)), dma((2, 2, 3)), dma((2, Z - 1)), dma((2, Z - 1)),
    ]
    shapes = (
        jax.ShapeDtypeStruct((2 * RI, 2 * CJ, CH), BF16),
        jax.ShapeDtypeStruct((RI * CJ, CH), BF16),
        jax.ShapeDtypeStruct((CB, FB), F32),
        jax.ShapeDtypeStruct((CB, FB), F32),
    )
    inputs = (coarse, skip, up_weight.reshape(9 * CH, CH), conv_weight.reshape(9 * CH, CH), cotangent)
    inputs = [pltpu.with_memory_space_constraint(x, pltpu.HBM) for x in inputs]
    results = pl.pallas_call(
        functools.partial(kernel, dims),
        out_shape=shapes,
        in_specs=[hbm] * 5,
        out_specs=(vmem,) * 4,
        scratch_shapes=scratch,
        compiler_params=pltpu.CompilerParams(
            collective_id=0, has_side_effects=True, vmem_limit_bytes=36 * 2**20
        ),
    )(*inputs)
    decoded, grad_coarse, grad_up, grad_conv = pl.pallas_call(
        deliver,
        out_shape=shapes,
        in_specs=[vmem] * 4,
        out_specs=(hbm,) * 4,
        scratch_shapes=[dma((4,))],
        compiler_params=pltpu.CompilerParams(vmem_limit_bytes=4 * 2**20),
    )(*results)
    return decoded, grad_coarse.reshape(RI, CJ, CH), grad_up.T, grad_conv.T


def build(mesh, dims):
    cells = P("band", "face", None)
    return jax.shard_map(
        functools.partial(local, dims),
        mesh=mesh,
        in_specs=(cells, cells, P(), P(), cells),
        out_specs=(cells, cells, P("face", "band"), P("face", "band")),
        check_vma=False,
    )


def solution(mesh):
    return build(mesh, (2, 4, 8, 2))
```

```python
import functools

import jax
import jax.numpy as jnp
from jax import lax
from jax.experimental import pallas as pl
from jax.experimental.pallas import tpu as pltpu
from jax.sharding import PartitionSpec as P

F32, BF16 = jnp.float32, jnp.bfloat16
MESH = pl.DeviceIdType.MESH
CH = 256
RI, CJ = 12, 16
XR, XC = 18, 32
AREA = XR * XC

UP1, UP2 = (0, 5, 6), (1, 2)
DOWN1, DOWN2 = (7, 8), (0, 3, 4, 5, 6)
LEFT1, LEFT2 = (0, 5, 7), (1, 3)
RIGHT1, RIGHT2 = (6, 8), (0, 2, 4, 5, 7)
CORNERS = (
    (-1, -1, (0, 1, 5)),
    (-1, 1, (0, 2, 5, 6)),
    (1, -1, (0, 3, 5, 7)),
    (1, 1, (0, 4, 5, 6, 7, 8)),
)
TAPS = [(k, l) for k in range(3) for l in range(3)]


def split(e):
    return e % 2, e // 2


def dot(a, b):
    return jnp.dot(a, b, preferred_element_type=F32)


def ld(ref, at, n, stride=1):
    if stride == 1:
        return jnp.concatenate([ref[h, pl.ds(at, n), :] for h in range(2)], axis=-1)
    return jnp.concatenate([ref[h, pl.ds(at, n, stride=stride), :] for h in range(2)], axis=-1)


def st(ref, at, n, value, stride=1):
    for h in range(2):
        part = value[:, 128 * h : 128 * h + 128]
        if stride == 1:
            ref[h, pl.ds(at, n), :] = part
        else:
            ref[h, pl.ds(at, n, stride=stride), :] = part


def far(n):
    return sorted(range(1, n), key=lambda d: (-min(d, n - d), d))


def kernel(
    dims,
    coarse_h, skip_h, upw_h, convw_h, cot_h,
    dec_o, gc_o, gu_o, gw_o,
    coarse_v, skip_v, cot_v, upw, convw, upwt, convwt,
    xf, fs, ft, af, gf, dfac, dghost, ce, cg, tv, tvp, av, gv, actt, dec_v,
    m_1, m_2, m_co, r_1, r_2, r_co,
    gsum, r0, s1, r1a, r1b, a1a, a1b, s2a, s2b, r2a, r2b, pad, a3, s3, r3,
    in_sem, hs, hr, s0s, s0r, s1s, s1r, s2s, s2r, s3s, s3r,
):
    loads = [
        pltpu.make_async_copy(src, dst, in_sem.at[n])
        for n, (src, dst) in enumerate(
            ((coarse_h, coarse_v), (cot_h, cot_v), (skip_h, skip_v), (convw_h, convw), (upw_h, upw))
        )
    ]
    for c in loads:
        c.start()

    XH, Y, Z, XL = dims
    NX = XH * XL
    HL = CH // XL
    FB = 9 * CH // (XH * Y * 2)
    RA = FB // 16 * 5 // 9 * 16
    CB = CH // (Z * XL)
    nface, nband = XH * Y * 2, Z * XL
    face, band = lax.axis_index("face"), lax.axis_index("band")
    rem, div = lax.rem, lax.div
    core = rem(face, 2)
    yy = rem(div(face, 2), Y)
    xh = div(face, 2 * Y)
    xl = rem(band, XL)
    zz = div(band, XL)
    xx = xh * XL + xl

    def dev(xx_, yy_, core_, zz_):
        return {
            "face": div(xx_, XL) * (2 * Y) + yy_ * 2 + core_,
            "band": zz_ * XL + rem(xx_, XL),
        }

    def near(di, dj):
        return {"face": rem(face + dj + nface, nface), "band": rem(band + di + nband, nband)}

    def at_core():
        return dev(xx, yy, 1 - core, zz)

    def at_y(d):
        return dev(xx, rem(yy + d, Y), core, zz)

    def at_x(d):
        return dev(rem(xx + d, NX), yy, core, zz)

    def at_z(d):
        return dev(xx, yy, core, rem(zz + d, Z))

    ways = [(-1, 0), (1, 0), (0, -1), (0, 1), (-1, -1), (-1, 1), (1, -1), (1, 1)]
    far_z, far_y, far_x = far(Z), far(Y), far(NX)
    partners = [near(*w) for w in ways[4:]] + [at_z(d) for d in far_z]
    partners += [at_x(d) for d in far_x] + [at_y(d) for d in far_y]
    partners += [near(*w) for w in ways[:4]] + [at_core()]
    barrier = pltpu.get_barrier_semaphore()
    for p in partners:
        pl.semaphore_signal(barrier, inc=1, device_id=p, device_id_type=MESH)

    def rows(a, i, col, n):
        return ld(xf, a * AREA + (i + 2) * XC + 8 + col, n, XC)

    for c in loads[:3]:
        c.wait()

    def spread(i, carry):
        base = pl.multiple_of((i + 2) * XC + 8, 8)
        st(xf, base, CJ, coarse_v[i].astype(F32))
        for src, stage, first in ((skip_v, fs, 1), (cot_v, ft, 5)):
            for r in range(2):
                st(stage, r * 2 * CJ, 2 * CJ, src[2 * i + r].astype(F32))
            for r in range(2):
                for s in range(2):
                    part = ld(stage, r * 2 * CJ + s, CJ, 2)
                    st(xf, pl.multiple_of(base + (first + 2 * r + s) * AREA, 8), CJ, part)
        return carry

    lax.fori_loop(0, RI, spread, 0)

    def message(buf, fields, way):
        for n, a in enumerate(fields):
            if way < 2:
                buf[way, n] = ld(xf, a * AREA + (2 if way == 0 else RI + 1) * XC + 8, CJ).astype(BF16)
            else:
                buf[way, n] = rows(a, 0, 0 if way == 2 else CJ - 1, 16).astype(BF16)

    for way, fields in enumerate((UP1, DOWN1, LEFT1, RIGHT1)):
        message(m_1, fields, way)
    for m, (di, dj, fields) in enumerate(CORNERS):
        for n, a in enumerate(fields):
            at = a * AREA + (2 + (0 if di < 0 else RI - 1)) * XC + 8 + (0 if dj < 0 else CJ - 1)
            m_co[m, n : n + 1] = ld(xf, at, 1)

    pl.semaphore_wait(barrier, len(partners))

    def remote(src, dst, ssem, rsem, to):
        return pltpu.make_async_remote_copy(
            src_ref=src, dst_ref=dst, send_sem=ssem, recv_sem=rsem, device_id=to, device_id_type=MESH
        )

    halo1, halo2 = [], []
    for m, (di, dj, _) in enumerate(CORNERS):
        halo1.append(remote(m_co.at[m], r_co.at[m], hs.at[m], hr.at[m], near(di, dj)))
    for way, fields in enumerate((UP1, DOWN1, LEFT1, RIGHT1)):
        n = len(fields)
        halo1.append(
            remote(m_1.at[way, :n], r_1.at[way, :n], hs.at[4 + way], hr.at[4 + way], near(*ways[way]))
        )
    for c in halo1:
        c.start()
    for way, fields in enumerate((UP2, DOWN2, LEFT2, RIGHT2)):
        message(m_2, fields, way)
        n = len(fields)
        halo2.append(
            remote(m_2.at[way, :n], r_2.at[way, :n], hs.at[8 + way], hr.at[8 + way], near(*ways[way]))
        )
    for c in halo2:
        c.start()

    for c in loads[3:]:
        c.wait()

    def turn(t, carry):
        at = pl.multiple_of(t * CH, CH)
        convwt[pl.ds(at, CH), :] = convw[pl.ds(at, CH), :].T
        upwt[pl.ds(at, CH), :] = upw[pl.ds(at, CH), :].T
        return carry

    lax.fori_loop(0, 9, turn, 0)
    src = lax.broadcasted_iota(jnp.int32, (CH, CH), 0)
    dst = lax.broadcasted_iota(jnp.int32, (CH, CH), 1)
    wanted = (((dst % HL) // CB) * XL + dst // HL) * CB + dst % CB
    perm = jnp.where(src == wanted, 1.0, 0.0).astype(BF16)

    keep_top = jnp.where(band == 0, 0.0, 1.0)
    keep_bot = jnp.where(band == nband - 1, 0.0, 1.0)

    def receive(buf, fields, way):
        for n, a in enumerate(fields):
            value = buf[way, n].astype(F32)
            if way == 0:
                st(xf, a * AREA + (RI + 2) * XC + 8, CJ, value * keep_bot)
            elif way == 1:
                st(xf, a * AREA + XC + 8, CJ, value * keep_top)
            else:
                st(xf, a * AREA + 2 * XC + (8 + CJ if way == 2 else 7), RI, value[:RI], XC)

    for c in halo1:
        c.wait()
    for way, fields in enumerate((UP1, DOWN1, LEFT1, RIGHT1)):
        receive(r_1, fields, way)
    for m, (di, dj, fields) in enumerate(CORNERS):
        keep = keep_bot if di < 0 else keep_top
        for n, a in enumerate(fields):
            at = a * AREA + (RI + 2 if di < 0 else 1) * XC + (8 + CJ if dj < 0 else 7)
            st(xf, at, 1, r_co[m, n : n + 1] * keep)

    def window(ref, a, i, dj, n):
        return jnp.concatenate(
            [ld(ref, a * AREA + (i + q + 2) * XC + 8 + dj, CJ) for q in range(n)], axis=0
        )

    def up(left, r, s):
        total = None
        for k, di in ((1, 0),) if r == 0 else ((2, 0), (0, 1)):
            for l, dj in ((1, 0),) if s == 0 else ((2, 0), (0, 1)):
                term = dot(left[2 * di + dj], upw[(3 * k + l) * CH : (3 * k + l + 1) * CH, :])
                total = term if total is None else total + term
        return total

    for di in range(2):
        for dj in range(2):
            ce[2 * di + dj] = window(xf, 0, di, dj, RI).astype(BF16)
    for r in range(2):
        for s in range(2):
            ph = 2 * r + s
            pre = up(ce, r, s) + window(xf, 1 + ph, 0, 0, RI)
            sig = jax.nn.sigmoid(pre)
            act = (pre * sig).astype(BF16).astype(F32)
            dfac[ph] = sig * (1.0 + pre * (1.0 - sig))
            for q in range(RI):
                st(af, ph * AREA + (q + 2) * XC + 8, CJ, act[16 * q : 16 * q + 16])
            actt[:, ph * 192 : ph * 192 + 192] = act.T.astype(BF16)

    for r in range(2):
        for s in range(2):
            for v, dj in enumerate((0, 1 if s == 0 else -1)):
                n = (2 * r + s) * 2 + v
                tv[n] = window(xf, 5 + 2 * r + s, -1, dj, 14).astype(BF16)
                tvp[n] = dot(tv[n], perm).astype(BF16)

    def view(ref, er, es, i0, n):
        (r, di), (s, dj) = split(er), split(es)
        at = (i0 + di + 1) * 16
        return ref[(2 * r + s) * 2 + (1 if dj else 0), at : at + 16 * n]

    def put(arr, t, value):
        start = t * CH
        while start < (t + 1) * CH:
            f, off = divmod(start, FB)
            stop = min((t + 1) * CH, (f + 1) * FB)
            gsum[arr, f // (2 * Y), (f // 2) % Y, f % 2, off : off + stop - start] = value[
                start - t * CH : stop - t * CH
            ]
            start = stop

    def first(arr, a):
        c = remote(gsum.at[arr, a, :, 1 - core], r0.at[arr, a], s0s.at[arr, a], s0r.at[arr, a], at_core())
        c.start()
        return c

    step0c = []
    for t, (k, l) in enumerate(TAPS):
        right = jnp.concatenate(
            [view(tvp, r - k + 1, s - l + 1, 0, RI) for r in range(2) for s in range(2)], axis=0
        )
        put(0, t, dot(actt[...], right).astype(BF16))
        if XH == 2 and t == 4:
            step0c.append(first(0, 0))
    step0c.append(first(0, XH - 1))

    for c in halo2:
        c.wait()
    for way, fields in enumerate((UP2, DOWN2, LEFT2, RIGHT2)):
        receive(r_2, fields, way)

    def border(a, di, dj):
        return jnp.concatenate(
            [window(xf, a, di - 1, dj, 1), window(xf, a, di + RI, dj, 1)]
            + [rows(a, di - 1, dj - 1, 16), rows(a, di - 1, dj + CJ, 16)],
            axis=0,
        )

    for di in range(2):
        for dj in range(2):
            cg[2 * di + dj] = border(0, di, dj).astype(BF16)
    line = lax.broadcasted_iota(jnp.int32, (64, CH), 0)
    first_row = (line < 16) | ((line >= 32) & (line % 16 == 0))
    last_row = ((line >= 16) & (line < 32)) | ((line >= 32) & (line % 16 == RI + 1))
    ghost = ((band == 0) & first_row) | ((band == nband - 1) & last_row)
    for r in range(2):
        for s in range(2):
            ph = 2 * r + s
            pre = up(cg, r, s) + border(1 + ph, 0, 0)
            sig = jax.nn.sigmoid(pre)
            act = jnp.where(ghost, 0.0, pre * sig).astype(BF16).astype(F32)
            dghost[ph] = jnp.where(ghost, 0.0, sig * (1.0 + pre * (1.0 - sig)))
            st(af, ph * AREA + XC + 8, CJ, act[:16])
            st(af, ph * AREA + (RI + 2) * XC + 8, CJ, act[16:32])
            st(af, ph * AREA + XC + 7, 16, act[32:48], XC)
            st(af, ph * AREA + XC + 8 + CJ, 16, act[48:], XC)

    for s in range(2):
        for v, dj in enumerate((0, 1 if s == 0 else -1)):
            tv[2 * s + v, :16] = window(xf, 5 + s, -1, dj, 1).astype(BF16)

    for r in range(2):
        for s in range(2):
            ph = 2 * r + s
            i0 = -1 if r else 0
            n = RI - i0
            left = jnp.concatenate([view(tv, r - k + 1, s - l + 1, i0, n) for k, l in TAPS], axis=1)
            if s:
                column = []
                for k, l in TAPS:
                    (r2, di), (s2, dj) = split(r - k + 1), split(s - l + 1)
                    column.append(rows(5 + 2 * r2 + s2, -1 + di, -1 + dj, 16).astype(BF16))
                left = jnp.concatenate([left, jnp.concatenate(column, axis=1)], axis=0)
            grad = dot(left, convwt[...])
            slope = jnp.concatenate([dghost[ph, :16], dfac[ph]], axis=0) if r else dfac[ph]
            main = (grad[: 16 * n] * slope).astype(BF16).astype(F32)
            for q in range(n):
                st(gf, ph * AREA + (i0 + q + 2) * XC + 8, CJ, main[16 * q : 16 * q + 16])
            if s:
                side = (grad[16 * n :] * dghost[ph, 32:48]).astype(BF16).astype(F32)
                st(gf, ph * AREA + XC + 7, 16, side, XC)

    coarse_t = window(xf, 0, 0, 0, RI).T.astype(BF16)
    step0u = []
    for t, (k, l) in enumerate(TAPS):
        (r, di), (s, dj) = split(k - 1), split(l - 1)
        part = window(gf, 2 * r + s, di, dj, RI).astype(BF16)
        gv[:, t * CH : (t + 1) * CH] = part
        put(1, t, dot(coarse_t, dot(part, perm).astype(BF16)).astype(BF16))
        if XH == 2 and t == 4:
            step0u.append(first(1, 0))
    step0u.append(first(1, XH - 1))

    def half(x2):
        return pl.ds(pl.multiple_of(rem(x2, XL) * HL, HL), HL)

    def stage1(arr, arrived):
        steps = [[], []]
        for a in range(XH):
            arrived[a].wait()
            for b in range(Y):
                total = gsum[arr, a, b, core].astype(F32) + r0[arr, a, b].astype(F32)
                s1[arr, a, b] = total.astype(BF16)
            for d in far_y:
                q = Y - d - 1
                steps[0].append(
                    remote(
                        s1.at[arr, a, rem(yy + d, Y), :RA], r1a.at[arr, q, a],
                        s1s.at[arr, a, d - 1], s1r.at[arr, a, q], at_y(d),
                    )
                )
                steps[0][-1].start()
        for d in far_x:
            q, x2 = NX - d - 1, rem(xx + d, NX)
            steps[1].append(
                remote(
                    s1.at[arr, div(x2, XL), :, RA:, half(x2)], r1b.at[arr, q],
                    s1s.at[arr, 2, d - 1], s1r.at[arr, 2, q], at_x(d),
                )
            )
            steps[1][-1].start()
        return steps

    def stage2a(arr, steps):
        for c in steps:
            c.wait()
        for a in range(XH):
            total = gsum[arr, a, yy, core, :RA].astype(F32) + r0[arr, a, yy, :RA].astype(F32)
            for d in range(Y - 1):
                total = total + r1a[arr, d, a].astype(F32)
            a1a[arr, a] = total
            s2a[arr, a] = total.astype(BF16)
        out = []
        for d in far_x:
            q, x2 = NX - d - 1, rem(xx + d, NX)
            out.append(
                remote(
                    s2a.at[arr, div(x2, XL), :, half(x2)], r2a.at[arr, q],
                    s2s.at[arr, 0, d - 1], s2r.at[arr, 0, q], at_x(d),
                )
            )
            out[-1].start()
        return out

    def stage2b(arr, steps):
        for c in steps:
            c.wait()
        own = half(xx)
        for b in range(Y):
            total = gsum[arr, xh, b, core, RA:, own].astype(F32) + r0[arr, xh, b, RA:, own].astype(F32)
            for d in range(NX - 1):
                total = total + r1b[arr, d, b].astype(F32)
            a1b[arr, b] = total
            s2b[arr, b] = total.astype(BF16)
        out = []
        for d in far_y:
            q = Y - d - 1
            out.append(
                remote(
                    s2b.at[arr, rem(yy + d, Y)], r2b.at[arr, q],
                    s2s.at[arr, 1, d - 1], s2r.at[arr, 1, q], at_y(d),
                )
            )
            out[-1].start()
        return out

    def stage3(arr, steps):
        for c in steps[0]:
            c.wait()
        total = a1a[arr, xh, :, half(xx)]
        for d in range(NX - 1):
            total = total + r2a[arr, d].astype(F32)
        pad[arr, :RA] = total
        for c in steps[1]:
            c.wait()
        total = a1b[arr, yy]
        for d in range(Y - 1):
            total = total + r2b[arr, d].astype(F32)
        pad[arr, RA:FB] = total
        turned = pad[arr].T
        for z in range(Z):
            a3[arr, z] = turned[z * CB : (z + 1) * CB]
            s3[arr, z] = turned[z * CB : (z + 1) * CB].astype(BF16)
        out = []
        for d in far_z:
            q = Z - d - 1
            out.append(
                remote(s3.at[arr, rem(zz + d, Z)], r3.at[arr, q], s3s.at[arr, d - 1], s3r.at[arr, q], at_z(d))
            )
            out[-1].start()
        return out

    def finish(arr, steps, out):
        for c in steps:
            c.wait()
        total = a3[arr, zz]
        for d in range(Z - 1):
            total = total + r3[arr, d].astype(F32)
        out[...] = total[:, :FB]

    def decode(r, s):
        left = jnp.concatenate([view(av, r + k - 1, s + l - 1, 0, RI) for k, l in TAPS], axis=1)
        out = dot(left, convw[...])
        for i in range(RI):
            st(dec_v, (2 * i + r) * 2 * CJ + s, CJ, out[16 * i : 16 * i + 16], 2)

    step1c = stage1(0, step0c)

    for r in range(2):
        for s in range(2):
            for v, dj in enumerate((0, 1 if s == 0 else -1)):
                av[(2 * r + s) * 2 + v] = window(af, 2 * r + s, -1, dj, 14).astype(BF16)

    step1u = stage1(1, step0u)

    decode(0, 0)
    decode(0, 1)
    decode(1, 0)
    decode(1, 1)
    gc_o[...] = dot(gv[...], upwt[...]).astype(BF16)
    for p in range(2 * RI):
        dec_o[p] = ld(dec_v, p * 2 * CJ, 2 * CJ).astype(BF16)

    step2c = [stage2a(0, step1c[0]), stage2b(0, step1c[1])]
    step2u = [stage2a(1, step1u[0]), stage2b(1, step1u[1])]
    step3c = stage3(0, step2c)
    step3u = stage3(1, step2u)
    finish(0, step3c, gw_o)
    finish(1, step3u, gu_o)


def deliver(*refs):
    n = (len(refs) - 1) // 2
    copies = [pltpu.make_async_copy(refs[i], refs[n + i], refs[-1].at[i]) for i in range(n)]
    for c in copies:
        c.start()
    for c in copies:
        c.wait()


def local(dims, coarse, skip, up_weight, conv_weight, cotangent):
    XH, Y, Z, XL = dims
    NX, HL = XH * XL, CH // XL
    FB, CB = 9 * CH // (XH * Y * 2), CH // (Z * XL)
    RA = FB // 16 * 5 // 9 * 16
    RB = FB - RA
    FP = -(-FB // 128) * 128
    hbm, vmem = pl.BlockSpec(memory_space=pltpu.HBM), pl.BlockSpec(memory_space=pltpu.VMEM)
    V, dma = pltpu.VMEM, pltpu.SemaphoreType.DMA
    wide = V((9 * CH, CH), BF16)
    scratch = [
        V((RI, CJ, CH), BF16), V((2 * RI, 2 * CJ, CH), BF16), V((2 * RI, 2 * CJ, CH), BF16),
        wide, wide, wide, wide,
        V((2, 9 * AREA, 128), F32), V((2, 4 * CJ, 128), F32), V((2, 4 * CJ, 128), F32),
        V((2, 4 * AREA, 128), F32), V((2, 4 * AREA, 128), F32), V((4, 192, CH), F32), V((4, 64, CH), F32),
        V((4, 192, CH), BF16), V((4, 64, CH), BF16),
        V((8, 224, CH), BF16), V((8, 224, CH), BF16), V((8, 224, CH), BF16),
        V((192, 9 * CH), BF16), V((CH, 768), BF16), V((2, 4 * RI * CJ, 128), F32),
        V((4, 3, 16, CH), BF16), V((4, 5, 16, CH), BF16), V((4, 8, CH), F32),
        V((4, 3, 16, CH), BF16), V((4, 5, 16, CH), BF16), V((4, 8, CH), F32),
        V((2, XH, Y, 2, FB, CH), BF16), V((2, XH, Y, FB, CH), BF16), V((2, XH, Y, FB, CH), BF16),
        V((2, Y - 1, XH, RA, CH), BF16), V((2, NX - 1, Y, RB, HL), BF16),
        V((2, XH, RA, CH), F32), V((2, Y, RB, HL), F32), V((2, XH, RA, CH), BF16), V((2, Y, RB, HL), BF16),
        V((2, NX - 1, RA, HL), BF16), V((2, Y - 1, RB, HL), BF16),
        V((2, FP, HL), F32), V((2, Z, CB, FP), F32), V((2, Z, CB, FP), BF16), V((2, Z - 1, CB, FP), BF16),
        dma((5,)), dma((12,)), dma((12,)), dma((2, 2)), dma((2, 2)),
        dma((2, 3, 3)), dma((2, 3, 3)), dma((2, 2, 3)), dma((2, 2, 3)), dma((2, Z - 1)), dma((2, Z - 1)),
    ]
    shapes = (
        jax.ShapeDtypeStruct((2 * RI, 2 * CJ, CH), BF16),
        jax.ShapeDtypeStruct((RI * CJ, CH), BF16),
        jax.ShapeDtypeStruct((CB, FB), F32),
        jax.ShapeDtypeStruct((CB, FB), F32),
    )
    inputs = (coarse, skip, up_weight.reshape(9 * CH, CH), conv_weight.reshape(9 * CH, CH), cotangent)
    inputs = [pltpu.with_memory_space_constraint(x, pltpu.HBM) for x in inputs]
    results = pl.pallas_call(
        functools.partial(kernel, dims),
        out_shape=shapes,
        in_specs=[hbm] * 5,
        out_specs=(vmem,) * 4,
        scratch_shapes=scratch,
        compiler_params=pltpu.CompilerParams(
            collective_id=0, has_side_effects=True, vmem_limit_bytes=36 * 2**20
        ),
    )(*inputs)
    decoded, grad_coarse, grad_up, grad_conv = pl.pallas_call(
        deliver,
        out_shape=shapes,
        in_specs=[vmem] * 4,
        out_specs=(hbm,) * 4,
        scratch_shapes=[dma((4,))],
        compiler_params=pltpu.CompilerParams(vmem_limit_bytes=4 * 2**20),
    )(*results)
    return decoded, grad_coarse.reshape(RI, CJ, CH), grad_up.T, grad_conv.T


def build(mesh, dims):
    cells = P("band", "face", None)
    return jax.shard_map(
        functools.partial(local, dims),
        mesh=mesh,
        in_specs=(cells, cells, P(), P(), cells),
        out_specs=(cells, cells, P("face", "band"), P("face", "band")),
        check_vma=False,
    )


def solution(mesh):
    return build(mesh, (2, 4, 8, 2))
```

```python
import functools

import jax
import jax.numpy as jnp
from jax import lax
from jax.experimental import pallas as pl
from jax.experimental.pallas import tpu as pltpu
from jax.sharding import PartitionSpec as P

F32, BF16 = jnp.float32, jnp.bfloat16
MESH = pl.DeviceIdType.MESH
CH = 256
RI, CJ = 12, 16
XR, XC = 18, 32
AREA = XR * XC

UP1, UP2 = (0, 5, 6), (1, 2)
DOWN1, DOWN2 = (7, 8), (0, 3, 4, 5, 6)
LEFT1, LEFT2 = (0, 5, 7), (1, 3)
RIGHT1, RIGHT2 = (6, 8), (0, 2, 4, 5, 7)
CORNERS = (
    (-1, -1, (0, 1, 5)),
    (-1, 1, (0, 2, 5, 6)),
    (1, -1, (0, 3, 5, 7)),
    (1, 1, (0, 4, 5, 6, 7, 8)),
)
TAPS = [(k, l) for k in range(3) for l in range(3)]


def split(e):
    return e % 2, e // 2


def dot(a, b):
    return jnp.dot(a, b, preferred_element_type=F32)


def ld(ref, at, n, stride=1):
    if stride == 1:
        return jnp.concatenate([ref[h, pl.ds(at, n), :] for h in range(2)], axis=-1)
    return jnp.concatenate([ref[h, pl.ds(at, n, stride=stride), :] for h in range(2)], axis=-1)


def st(ref, at, n, value, stride=1):
    for h in range(2):
        part = value[:, 128 * h : 128 * h + 128]
        if stride == 1:
            ref[h, pl.ds(at, n), :] = part
        else:
            ref[h, pl.ds(at, n, stride=stride), :] = part


def far(n):
    return sorted(range(1, n), key=lambda d: (-min(d, n - d), d))


def kernel(
    dims,
    coarse_h, skip_h, upw_h, convw_h, cot_h,
    dec_o, gc_o, gu_o, gw_o,
    coarse_v, skip_v, cot_v, upw, convw, upwt, convwt,
    xf, fs, ft, af, gf, dfac, dghost, ce, cg, cet, gpp, gb, tv, tvp, av, gv, actt, dec_v,
    m_1, m_2, m_co, r_1, r_2, r_co,
    gsum, r0, s1, r1a, r1b, a1a, a1b, s2a, s2b, r2a, r2b, pad, a3, s3, r3,
    in_sem, hs, hr, s0s, s0r, s1s, s1r, s2s, s2r, s3s, s3r,
):
    loads = [
        pltpu.make_async_copy(src, dst, in_sem.at[n])
        for n, (src, dst) in enumerate(
            ((coarse_h, coarse_v), (cot_h, cot_v), (skip_h, skip_v), (convw_h, convw), (upw_h, upw))
        )
    ]
    for c in loads:
        c.start()

    XH, Y, Z, XL = dims
    NX = XH * XL
    HL = CH // XL
    FB = 9 * CH // (XH * Y * 2)
    RA = FB // 16 * 5 // 9 * 16
    CB = CH // (Z * XL)
    nface, nband = XH * Y * 2, Z * XL
    face, band = lax.axis_index("face"), lax.axis_index("band")
    rem, div = lax.rem, lax.div
    core = rem(face, 2)
    yy = rem(div(face, 2), Y)
    xh = div(face, 2 * Y)
    xl = rem(band, XL)
    zz = div(band, XL)
    xx = xh * XL + xl

    def dev(xx_, yy_, core_, zz_):
        return {
            "face": div(xx_, XL) * (2 * Y) + yy_ * 2 + core_,
            "band": zz_ * XL + rem(xx_, XL),
        }

    def near(di, dj):
        return {"face": rem(face + dj + nface, nface), "band": rem(band + di + nband, nband)}

    def at_core():
        return dev(xx, yy, 1 - core, zz)

    def at_y(d):
        return dev(xx, rem(yy + d, Y), core, zz)

    def at_x(d):
        return dev(rem(xx + d, NX), yy, core, zz)

    def at_z(d):
        return dev(xx, yy, core, rem(zz + d, Z))

    ways = [(-1, 0), (1, 0), (0, -1), (0, 1), (-1, -1), (-1, 1), (1, -1), (1, 1)]
    far_z, far_y, far_x = far(Z), far(Y), far(NX)
    partners = [near(*w) for w in ways[4:]] + [at_z(d) for d in far_z]
    partners += [at_x(d) for d in far_x] + [at_y(d) for d in far_y]
    partners += [near(*w) for w in ways[:4]] + [at_core()]
    barrier = pltpu.get_barrier_semaphore()
    for p in partners:
        pl.semaphore_signal(barrier, inc=1, device_id=p, device_id_type=MESH)

    def rows(a, i, col, n):
        return ld(xf, a * AREA + (i + 2) * XC + 8 + col, n, XC)

    for c in loads[:3]:
        c.wait()

    def spread(i, carry):
        base = pl.multiple_of((i + 2) * XC + 8, 8)
        st(xf, base, CJ, coarse_v[i].astype(F32))
        for src, stage, first in ((skip_v, fs, 1), (cot_v, ft, 5)):
            for r in range(2):
                st(stage, r * 2 * CJ, 2 * CJ, src[2 * i + r].astype(F32))
            for r in range(2):
                for s in range(2):
                    part = ld(stage, r * 2 * CJ + s, CJ, 2)
                    st(xf, pl.multiple_of(base + (first + 2 * r + s) * AREA, 8), CJ, part)
        return carry

    lax.fori_loop(0, RI, spread, 0)

    def message(buf, fields, way):
        for n, a in enumerate(fields):
            if way < 2:
                buf[way, n] = ld(xf, a * AREA + (2 if way == 0 else RI + 1) * XC + 8, CJ).astype(BF16)
            else:
                buf[way, n] = rows(a, 0, 0 if way == 2 else CJ - 1, 16).astype(BF16)

    for way, fields in enumerate((UP1, DOWN1, LEFT1, RIGHT1)):
        message(m_1, fields, way)
    for m, (di, dj, fields) in enumerate(CORNERS):
        for n, a in enumerate(fields):
            at = a * AREA + (2 + (0 if di < 0 else RI - 1)) * XC + 8 + (0 if dj < 0 else CJ - 1)
            m_co[m, n : n + 1] = ld(xf, at, 1)

    pl.semaphore_wait(barrier, len(partners))

    def remote(src, dst, ssem, rsem, to):
        return pltpu.make_async_remote_copy(
            src_ref=src, dst_ref=dst, send_sem=ssem, recv_sem=rsem, device_id=to, device_id_type=MESH
        )

    halo1, halo2 = [], []
    for m, (di, dj, _) in enumerate(CORNERS):
        halo1.append(remote(m_co.at[m], r_co.at[m], hs.at[m], hr.at[m], near(di, dj)))
    for way, fields in enumerate((UP1, DOWN1, LEFT1, RIGHT1)):
        n = len(fields)
        halo1.append(
            remote(m_1.at[way, :n], r_1.at[way, :n], hs.at[4 + way], hr.at[4 + way], near(*ways[way]))
        )
    for c in halo1:
        c.start()
    for c in loads[3:]:
        c.wait()

    def turn(t, carry):
        at = pl.multiple_of(t * CH, CH)
        convwt[pl.ds(at, CH), :] = convw[pl.ds(at, CH), :].T
        upwt[pl.ds(at, CH), :] = upw[pl.ds(at, CH), :].T
        return carry

    lax.fori_loop(0, 9, turn, 0)
    src = lax.broadcasted_iota(jnp.int32, (CH, CH), 0)
    dst = lax.broadcasted_iota(jnp.int32, (CH, CH), 1)
    wanted = (((dst % HL) // CB) * XL + dst // HL) * CB + dst % CB
    perm = jnp.where(src == wanted, 1.0, 0.0).astype(BF16)

    keep_top = jnp.where(band == 0, 0.0, 1.0)
    keep_bot = jnp.where(band == nband - 1, 0.0, 1.0)

    def receive(buf, fields, way):
        for n, a in enumerate(fields):
            value = buf[way, n].astype(F32)
            if way == 0:
                st(xf, a * AREA + (RI + 2) * XC + 8, CJ, value * keep_bot)
            elif way == 1:
                st(xf, a * AREA + XC + 8, CJ, value * keep_top)
            else:
                st(xf, a * AREA + 2 * XC + (8 + CJ if way == 2 else 7), RI, value[:RI], XC)

    for way, fields in enumerate((UP2, DOWN2, LEFT2, RIGHT2)):
        message(m_2, fields, way)
        n = len(fields)
        halo2.append(
            remote(m_2.at[way, :n], r_2.at[way, :n], hs.at[8 + way], hr.at[8 + way], near(*ways[way]))
        )
    for c in halo1:
        c.wait()
    for c in halo2:
        c.start()
    for way, fields in enumerate((UP1, DOWN1, LEFT1, RIGHT1)):
        receive(r_1, fields, way)
    for m, (di, dj, fields) in enumerate(CORNERS):
        keep = keep_bot if di < 0 else keep_top
        for n, a in enumerate(fields):
            at = a * AREA + (RI + 2 if di < 0 else 1) * XC + (8 + CJ if dj < 0 else 7)
            st(xf, at, 1, r_co[m, n : n + 1] * keep)

    def window(ref, a, i, dj, n):
        return jnp.concatenate(
            [ld(ref, a * AREA + (i + q + 2) * XC + 8 + dj, CJ) for q in range(n)], axis=0
        )

    def up(left, r, s):
        total = None
        for k, di in ((1, 0),) if r == 0 else ((2, 0), (0, 1)):
            for l, dj in ((1, 0),) if s == 0 else ((2, 0), (0, 1)):
                term = dot(left[2 * di + dj], upw[(3 * k + l) * CH : (3 * k + l + 1) * CH, :])
                total = term if total is None else total + term
        return total

    for di in range(2):
        for dj in range(2):
            ce[2 * di + dj] = window(xf, 0, di, dj, RI).astype(BF16)
    for r in range(2):
        for s in range(2):
            ph = 2 * r + s
            pre = up(ce, r, s) + window(xf, 1 + ph, 0, 0, RI)
            sig = jax.nn.sigmoid(pre)
            act = (pre * sig).astype(BF16).astype(F32)
            dfac[ph] = sig * (1.0 + pre * (1.0 - sig))
            for q in range(RI):
                st(af, ph * AREA + (q + 2) * XC + 8, CJ, act[16 * q : 16 * q + 16])
            actt[:, ph * 192 : ph * 192 + 192] = act.T.astype(BF16)

    for r in range(2):
        for s in range(2):
            for v, dj in enumerate((0, 1 if s == 0 else -1)):
                n = (2 * r + s) * 2 + v
                tv[n] = window(xf, 5 + 2 * r + s, -1, dj, 14).astype(BF16)
                tvp[n] = dot(tv[n], perm).astype(BF16)

    def view(ref, er, es, i0, n):
        (r, di), (s, dj) = split(er), split(es)
        at = (i0 + di + 1) * 16
        return ref[(2 * r + s) * 2 + (1 if dj else 0), at : at + 16 * n]

    def put(arr, t, value):
        start = t * CH
        while start < (t + 1) * CH:
            f, off = divmod(start, FB)
            stop = min((t + 1) * CH, (f + 1) * FB)
            gsum[arr, f // (2 * Y), (f // 2) % Y, f % 2, off : off + stop - start] = value[
                start - t * CH : stop - t * CH
            ]
            start = stop

    def first(arr, a):
        c = remote(gsum.at[arr, a, :, 1 - core], r0.at[arr, a], s0s.at[arr, a], s0r.at[arr, a], at_core())
        c.start()
        return c

    step0c = []
    for t, (k, l) in enumerate(TAPS):
        right = jnp.concatenate(
            [view(tvp, r - k + 1, s - l + 1, 0, RI) for r in range(2) for s in range(2)], axis=0
        )
        put(0, t, dot(actt[...], right).astype(BF16))
        if XH == 2 and t == 4:
            step0c.append(first(0, 0))
    step0c.append(first(0, XH - 1))

    def half(x2):
        return pl.ds(pl.multiple_of(rem(x2, XL) * HL, HL), HL)

    def stage1(arr, arrived):
        steps = [[], []]
        for a in range(XH):
            arrived[a].wait()
            for b in range(Y):
                total = gsum[arr, a, b, core].astype(F32) + r0[arr, a, b].astype(F32)
                s1[arr, a, b] = total.astype(BF16)
            for d in far_y:
                q = Y - d - 1
                steps[0].append(
                    remote(
                        s1.at[arr, a, rem(yy + d, Y), :RA], r1a.at[arr, q, a],
                        s1s.at[arr, a, d - 1], s1r.at[arr, a, q], at_y(d),
                    )
                )
                steps[0][-1].start()
        for d in far_x:
            q, x2 = NX - d - 1, rem(xx + d, NX)
            steps[1].append(
                remote(
                    s1.at[arr, div(x2, XL), :, RA:, half(x2)], r1b.at[arr, q],
                    s1s.at[arr, 2, d - 1], s1r.at[arr, 2, q], at_x(d),
                )
            )
            steps[1][-1].start()
        return steps

    phases = [(r, s) for r in range(2) for s in range(2)]

    def stacked(ref, step, group):
        return jnp.concatenate(
            [
                jnp.concatenate([view(ref, *step(r, s, k, l), 0, RI) for r, s in group], axis=0)
                for k, l in TAPS
            ],
            axis=1,
        )

    for g in range(0, 4, 4):
        group = phases[g : g + 4]
        left = stacked(tv, lambda r, s, k, l: (r - k + 1, s - l + 1), group)
        grads = dot(left, convwt[...])
        for n, (r, s) in enumerate(group):
            ph = 2 * r + s
            grad = (grads[192 * n : 192 * n + 192] * dfac[ph]).astype(BF16)
            gpp[ph] = dot(grad, perm).astype(BF16)
            gb[ph] = grad

    for n in range(4):
        cet[n] = window(xf, 0, n // 2, n % 2, RI).T.astype(BF16)
    step1c = stage1(0, step0c)
    step0u = []
    for t, (k, l) in enumerate(TAPS):
        (r, di), (s, dj) = (((1, 1), (0, 0), (1, 0))[m] for m in (k, l))
        put(1, t, dot(cet[2 * di + dj], gpp[2 * r + s]).astype(BF16))
        if XH == 2 and t == 4:
            step0u.append(first(1, 0))
    step0u.append(first(1, XH - 1))

    def stage2a(arr, steps):
        for c in steps:
            c.wait()
        for a in range(XH):
            total = gsum[arr, a, yy, core, :RA].astype(F32) + r0[arr, a, yy, :RA].astype(F32)
            for d in range(Y - 1):
                total = total + r1a[arr, d, a].astype(F32)
            a1a[arr, a] = total
            s2a[arr, a] = total.astype(BF16)
        out = []
        for d in far_x:
            q, x2 = NX - d - 1, rem(xx + d, NX)
            out.append(
                remote(
                    s2a.at[arr, div(x2, XL), :, half(x2)], r2a.at[arr, q],
                    s2s.at[arr, 0, d - 1], s2r.at[arr, 0, q], at_x(d),
                )
            )
            out[-1].start()
        return out

    def stage2b(arr, steps):
        for c in steps:
            c.wait()
        own = half(xx)
        for b in range(Y):
            total = gsum[arr, xh, b, core, RA:, own].astype(F32) + r0[arr, xh, b, RA:, own].astype(F32)
            for d in range(NX - 1):
                total = total + r1b[arr, d, b].astype(F32)
            a1b[arr, b] = total
            s2b[arr, b] = total.astype(BF16)
        out = []
        for d in far_y:
            q = Y - d - 1
            out.append(
                remote(
                    s2b.at[arr, rem(yy + d, Y)], r2b.at[arr, q],
                    s2s.at[arr, 1, d - 1], s2r.at[arr, 1, q], at_y(d),
                )
            )
            out[-1].start()
        return out

    def stage3(arr, steps):
        for c in steps[0]:
            c.wait()
        total = a1a[arr, xh, :, half(xx)]
        for d in range(NX - 1):
            total = total + r2a[arr, d].astype(F32)
        pad[arr, :RA] = total
        for c in steps[1]:
            c.wait()
        total = a1b[arr, yy]
        for d in range(Y - 1):
            total = total + r2b[arr, d].astype(F32)
        pad[arr, RA:FB] = total
        turned = pad[arr].T
        for z in range(Z):
            a3[arr, z] = turned[z * CB : (z + 1) * CB]
            s3[arr, z] = turned[z * CB : (z + 1) * CB].astype(BF16)
        out = []
        for d in far_z:
            q = Z - d - 1
            out.append(
                remote(s3.at[arr, rem(zz + d, Z)], r3.at[arr, q], s3s.at[arr, d - 1], s3r.at[arr, q], at_z(d))
            )
            out[-1].start()
        return out

    def finish(arr, steps, out):
        for c in steps:
            c.wait()
        total = a3[arr, zz]
        for d in range(Z - 1):
            total = total + r3[arr, d].astype(F32)
        out[...] = total[:, :FB]

    def decode(group):
        outs = dot(stacked(av, lambda r, s, k, l: (r + k - 1, s + l - 1), group), convw[...])
        for n, (r, s) in enumerate(group):
            out = outs[192 * n : 192 * n + 192]
            for i in range(RI):
                st(dec_v, (2 * i + r) * 2 * CJ + s, CJ, out[16 * i : 16 * i + 16], 2)

    step1u = stage1(1, step0u)

    for c in halo2:
        c.wait()
    for way, fields in enumerate((UP2, DOWN2, LEFT2, RIGHT2)):
        receive(r_2, fields, way)

    def border(a, di, dj):
        return jnp.concatenate(
            [window(xf, a, di - 1, dj, 1), window(xf, a, di + RI, dj, 1)]
            + [rows(a, di - 1, dj - 1, 16), rows(a, di - 1, dj + CJ, 16)],
            axis=0,
        )

    for di in range(2):
        for dj in range(2):
            cg[2 * di + dj] = border(0, di, dj).astype(BF16)
    line = lax.broadcasted_iota(jnp.int32, (64, CH), 0)
    first_row = (line < 16) | ((line >= 32) & (line % 16 == 0))
    last_row = ((line >= 16) & (line < 32)) | ((line >= 32) & (line % 16 == RI + 1))
    ghost = ((band == 0) & first_row) | ((band == nband - 1) & last_row)
    for r in range(2):
        for s in range(2):
            ph = 2 * r + s
            pre = up(cg, r, s) + border(1 + ph, 0, 0)
            sig = jax.nn.sigmoid(pre)
            act = jnp.where(ghost, 0.0, pre * sig).astype(BF16).astype(F32)
            dghost[ph] = jnp.where(ghost, 0.0, sig * (1.0 + pre * (1.0 - sig)))
            st(af, ph * AREA + XC + 8, CJ, act[:16])
            st(af, ph * AREA + (RI + 2) * XC + 8, CJ, act[16:32])
            st(af, ph * AREA + XC + 7, 16, act[32:48], XC)
            st(af, ph * AREA + XC + 8 + CJ, 16, act[48:], XC)

    for s in range(2):
        for v, dj in enumerate((0, 1 if s == 0 else -1)):
            tv[2 * s + v, :16] = window(xf, 5 + s, -1, dj, 1).astype(BF16)

    for r in range(2):
        for s in range(2):
            for v, dj in enumerate((0, 1 if s == 0 else -1)):
                av[(2 * r + s) * 2 + v] = window(af, 2 * r + s, -1, dj, 14).astype(BF16)

    for ph in range(4):
        grad = gb[ph].astype(F32)
        for q in range(RI):
            st(gf, ph * AREA + (q + 2) * XC + 8, CJ, grad[16 * q : 16 * q + 16])
    lines, slopes = [], []
    for s in range(2):
        lines.append(jnp.concatenate([view(tv, 2 - k, s - l + 1, -1, 1) for k, l in TAPS], axis=1))
        slopes.append(dghost[2 + s, :16])
    for r in range(2):
        column = []
        for k, l in TAPS:
            (r2, di), (s2, dj) = split(r - k + 1), split(2 - l)
            column.append(rows(5 + 2 * r2 + s2, -1 + di, -1 + dj, 16).astype(BF16))
        lines.append(jnp.concatenate(column, axis=1))
        slopes.append(dghost[2 * r + 1, 32:48])
    grad = dot(jnp.concatenate(lines, axis=0), convwt[...]) * jnp.concatenate(slopes, axis=0)
    grad = grad.astype(BF16).astype(F32)
    st(gf, 2 * AREA + XC + 8, CJ, grad[:16])
    st(gf, 3 * AREA + XC + 8, CJ, grad[16:32])
    st(gf, AREA + XC + 7, 16, grad[32:48], XC)
    st(gf, 3 * AREA + XC + 7, 16, grad[48:], XC)
    for t, (k, l) in enumerate(TAPS):
        (r, di), (s, dj) = split(k - 1), split(l - 1)
        gv[:, t * CH : (t + 1) * CH] = window(gf, 2 * r + s, di, dj, RI).astype(BF16)

    decode(phases[0:4])
    gc_o[...] = dot(gv[...], upwt[...]).astype(BF16)
    for p in range(2 * RI):
        dec_o[p] = ld(dec_v, p * 2 * CJ, 2 * CJ).astype(BF16)

    step2c = [stage2a(0, step1c[0]), stage2b(0, step1c[1])]
    step2u = [stage2a(1, step1u[0]), stage2b(1, step1u[1])]
    step3c = stage3(0, step2c)
    step3u = stage3(1, step2u)
    finish(0, step3c, gw_o)
    finish(1, step3u, gu_o)


def deliver(*refs):
    n = (len(refs) - 1) // 2
    copies = [pltpu.make_async_copy(refs[i], refs[n + i], refs[-1].at[i]) for i in range(n)]
    for c in copies:
        c.start()
    for c in copies:
        c.wait()


def local(dims, coarse, skip, up_weight, conv_weight, cotangent):
    XH, Y, Z, XL = dims
    NX, HL = XH * XL, CH // XL
    FB, CB = 9 * CH // (XH * Y * 2), CH // (Z * XL)
    RA = FB // 16 * 5 // 9 * 16
    RB = FB - RA
    FP = -(-FB // 128) * 128
    hbm, vmem = pl.BlockSpec(memory_space=pltpu.HBM), pl.BlockSpec(memory_space=pltpu.VMEM)
    V, dma = pltpu.VMEM, pltpu.SemaphoreType.DMA
    wide = V((9 * CH, CH), BF16)
    scratch = [
        V((RI, CJ, CH), BF16), V((2 * RI, 2 * CJ, CH), BF16), V((2 * RI, 2 * CJ, CH), BF16),
        wide, wide, wide, wide,
        V((2, 9 * AREA, 128), F32), V((2, 4 * CJ, 128), F32), V((2, 4 * CJ, 128), F32),
        V((2, 4 * AREA, 128), F32), V((2, 4 * AREA, 128), F32), V((4, 192, CH), F32), V((4, 64, CH), F32),
        V((4, 192, CH), BF16), V((4, 64, CH), BF16), V((4, CH, 192), BF16), V((4, 192, CH), BF16), V((4, 192, CH), BF16),
        V((8, 224, CH), BF16), V((8, 224, CH), BF16), V((8, 224, CH), BF16),
        V((192, 9 * CH), BF16), V((CH, 768), BF16), V((2, 4 * RI * CJ, 128), F32),
        V((4, 3, 16, CH), BF16), V((4, 5, 16, CH), BF16), V((4, 8, CH), F32),
        V((4, 3, 16, CH), BF16), V((4, 5, 16, CH), BF16), V((4, 8, CH), F32),
        V((2, XH, Y, 2, FB, CH), BF16), V((2, XH, Y, FB, CH), BF16), V((2, XH, Y, FB, CH), BF16),
        V((2, Y - 1, XH, RA, CH), BF16), V((2, NX - 1, Y, RB, HL), BF16),
        V((2, XH, RA, CH), F32), V((2, Y, RB, HL), F32), V((2, XH, RA, CH), BF16), V((2, Y, RB, HL), BF16),
        V((2, NX - 1, RA, HL), BF16), V((2, Y - 1, RB, HL), BF16),
        V((2, FP, HL), F32), V((2, Z, CB, FP), F32), V((2, Z, CB, FP), BF16), V((2, Z - 1, CB, FP), BF16),
        dma((5,)), dma((12,)), dma((12,)), dma((2, 2)), dma((2, 2)),
        dma((2, 3, 3)), dma((2, 3, 3)), dma((2, 2, 3)), dma((2, 2, 3)), dma((2, Z - 1)), dma((2, Z - 1)),
    ]
    shapes = (
        jax.ShapeDtypeStruct((2 * RI, 2 * CJ, CH), BF16),
        jax.ShapeDtypeStruct((RI * CJ, CH), BF16),
        jax.ShapeDtypeStruct((CB, FB), F32),
        jax.ShapeDtypeStruct((CB, FB), F32),
    )
    inputs = (coarse, skip, up_weight.reshape(9 * CH, CH), conv_weight.reshape(9 * CH, CH), cotangent)
    inputs = [pltpu.with_memory_space_constraint(x, pltpu.HBM) for x in inputs]
    results = pl.pallas_call(
        functools.partial(kernel, dims),
        out_shape=shapes,
        in_specs=[hbm] * 5,
        out_specs=(vmem,) * 4,
        scratch_shapes=scratch,
        compiler_params=pltpu.CompilerParams(
            collective_id=0, has_side_effects=True, vmem_limit_bytes=36 * 2**20
        ),
    )(*inputs)
    decoded, grad_coarse, grad_up, grad_conv = pl.pallas_call(
        deliver,
        out_shape=shapes,
        in_specs=[vmem] * 4,
        out_specs=(hbm,) * 4,
        scratch_shapes=[dma((4,))],
        compiler_params=pltpu.CompilerParams(vmem_limit_bytes=4 * 2**20),
    )(*results)
    return decoded, grad_coarse.reshape(RI, CJ, CH), grad_up.T, grad_conv.T


def build(mesh, dims):
    cells = P("band", "face", None)
    return jax.shard_map(
        functools.partial(local, dims),
        mesh=mesh,
        in_specs=(cells, cells, P(), P(), cells),
        out_specs=(cells, cells, P("face", "band"), P("face", "band")),
        check_vma=False,
    )


def solution(mesh):
    return build(mesh, (2, 4, 8, 2))
```

```python
import functools

import jax
import jax.numpy as jnp
from jax import lax
from jax.experimental import pallas as pl
from jax.experimental.pallas import tpu as pltpu
from jax.sharding import PartitionSpec as P

F32, BF16 = jnp.float32, jnp.bfloat16
MESH = pl.DeviceIdType.MESH
CH = 256
RI, CJ = 12, 16
XR, XC = 18, 32
AREA = XR * XC

UP1, UP2 = (0, 5, 6), (1, 2)
DOWN1, DOWN2 = (7, 8), (0, 3, 4, 5, 6)
LEFT1, LEFT2 = (0, 5, 7), (1, 3)
RIGHT1, RIGHT2 = (6, 8), (0, 2, 4, 5, 7)
CORNERS = (
    (-1, -1, (0, 1, 5)),
    (-1, 1, (0, 2, 5, 6)),
    (1, -1, (0, 3, 5, 7)),
    (1, 1, (0, 4, 5, 6, 7, 8)),
)
TAPS = [(k, l) for k in range(3) for l in range(3)]


def split(e):
    return e % 2, e // 2


def dot(a, b):
    return jnp.dot(a, b, preferred_element_type=F32)


def ld(ref, at, n, stride=1):
    if stride == 1:
        return jnp.concatenate([ref[h, pl.ds(at, n), :] for h in range(2)], axis=-1)
    return jnp.concatenate([ref[h, pl.ds(at, n, stride=stride), :] for h in range(2)], axis=-1)


def st(ref, at, n, value, stride=1):
    for h in range(2):
        part = value[:, 128 * h : 128 * h + 128]
        if stride == 1:
            ref[h, pl.ds(at, n), :] = part
        else:
            ref[h, pl.ds(at, n, stride=stride), :] = part


def far(n):
    return sorted(range(1, n), key=lambda d: (-min(d, n - d), d))


def kernel(
    dims,
    coarse_h, skip_h, upw_h, convw_h, cot_h,
    dec_o, gc_o, gu_o, gw_o,
    coarse_v, skip_v, cot_v, upw, convw, upwt, convwt,
    xf, fs, ft, af, gf, dfac, dghost, ce, cg, cet, gpp, gb, tv, tvp, av, gv, actt, dec_v,
    m_1, m_2, m_co, r_1, r_2, r_co,
    gsum, r0, s1, r1a, r1b, a1a, a1b, s2a, s2b, r2a, r2b, pad, a3, s3, r3,
    in_sem, hs, hr, s0s, s0r, s1s, s1r, s2s, s2r, s3s, s3r,
):
    loads = [
        pltpu.make_async_copy(src, dst, in_sem.at[n])
        for n, (src, dst) in enumerate(
            ((coarse_h, coarse_v), (cot_h, cot_v), (skip_h, skip_v), (convw_h, convw), (upw_h, upw))
        )
    ]
    for c in loads:
        c.start()

    XH, Y, Z, XL = dims
    NX = XH * XL
    HL = CH // XL
    FB = 9 * CH // (XH * Y * 2)
    RA = FB // 16 * 5 // 9 * 16
    CB = CH // (Z * XL)
    nface, nband = XH * Y * 2, Z * XL
    face, band = lax.axis_index("face"), lax.axis_index("band")
    rem, div = lax.rem, lax.div
    core = rem(face, 2)
    yy = rem(div(face, 2), Y)
    xh = div(face, 2 * Y)
    xl = rem(band, XL)
    zz = div(band, XL)
    xx = xh * XL + xl

    def dev(xx_, yy_, core_, zz_):
        return {
            "face": div(xx_, XL) * (2 * Y) + yy_ * 2 + core_,
            "band": zz_ * XL + rem(xx_, XL),
        }

    def near(di, dj):
        return {"face": rem(face + dj + nface, nface), "band": rem(band + di + nband, nband)}

    def at_core():
        return dev(xx, yy, 1 - core, zz)

    def at_y(d):
        return dev(xx, rem(yy + d, Y), core, zz)

    def at_x(d):
        return dev(rem(xx + d, NX), yy, core, zz)

    def at_z(d):
        return dev(xx, yy, core, rem(zz + d, Z))

    ways = [(-1, 0), (1, 0), (0, -1), (0, 1), (-1, -1), (-1, 1), (1, -1), (1, 1)]
    far_z, far_y, far_x = far(Z), far(Y), far(NX)
    partners = [near(*w) for w in ways[4:]] + [at_z(d) for d in far_z]
    partners += [at_x(d) for d in far_x] + [at_y(d) for d in far_y]
    partners += [near(*w) for w in ways[:4]] + [at_core()]
    barrier = pltpu.get_barrier_semaphore()
    for p in partners:
        pl.semaphore_signal(barrier, inc=1, device_id=p, device_id_type=MESH)

    def rows(a, i, col, n):
        return ld(xf, a * AREA + (i + 2) * XC + 8 + col, n, XC)

    for c in loads[:3]:
        c.wait()

    def spread(i, carry):
        base = pl.multiple_of((i + 2) * XC + 8, 8)
        st(xf, base, CJ, coarse_v[i].astype(F32))
        for src, stage, first in ((skip_v, fs, 1), (cot_v, ft, 5)):
            for r in range(2):
                st(stage, r * 2 * CJ, 2 * CJ, src[2 * i + r].astype(F32))
            for r in range(2):
                for s in range(2):
                    part = ld(stage, r * 2 * CJ + s, CJ, 2)
                    st(xf, pl.multiple_of(base + (first + 2 * r + s) * AREA, 8), CJ, part)
        return carry

    lax.fori_loop(0, RI, spread, 0)

    def message(buf, fields, way):
        for n, a in enumerate(fields):
            if way < 2:
                buf[way, n] = ld(xf, a * AREA + (2 if way == 0 else RI + 1) * XC + 8, CJ).astype(BF16)
            else:
                buf[way, n] = rows(a, 0, 0 if way == 2 else CJ - 1, 16).astype(BF16)

    for way, fields in enumerate((UP1, DOWN1, LEFT1, RIGHT1)):
        message(m_1, fields, way)
    for m, (di, dj, fields) in enumerate(CORNERS):
        for n, a in enumerate(fields):
            at = a * AREA + (2 + (0 if di < 0 else RI - 1)) * XC + 8 + (0 if dj < 0 else CJ - 1)
            m_co[m, n : n + 1] = ld(xf, at, 1)

    pl.semaphore_wait(barrier, len(partners))

    def remote(src, dst, ssem, rsem, to):
        return pltpu.make_async_remote_copy(
            src_ref=src, dst_ref=dst, send_sem=ssem, recv_sem=rsem, device_id=to, device_id_type=MESH
        )

    halo1, halo2 = [], []
    for m, (di, dj, _) in enumerate(CORNERS):
        halo1.append(remote(m_co.at[m], r_co.at[m], hs.at[m], hr.at[m], near(di, dj)))
    for way, fields in enumerate((UP1, DOWN1, LEFT1, RIGHT1)):
        n = len(fields)
        halo1.append(
            remote(m_1.at[way, :n], r_1.at[way, :n], hs.at[4 + way], hr.at[4 + way], near(*ways[way]))
        )
    for c in halo1:
        c.start()
    for c in loads[3:]:
        c.wait()

    def turn(t, carry):
        at = pl.multiple_of(t * CH, CH)
        convwt[pl.ds(at, CH), :] = convw[pl.ds(at, CH), :].T
        upwt[pl.ds(at, CH), :] = upw[pl.ds(at, CH), :].T
        return carry

    lax.fori_loop(0, 9, turn, 0)
    src = lax.broadcasted_iota(jnp.int32, (CH, CH), 0)
    dst = lax.broadcasted_iota(jnp.int32, (CH, CH), 1)
    wanted = (((dst % HL) // CB) * XL + dst // HL) * CB + dst % CB
    perm = jnp.where(src == wanted, 1.0, 0.0).astype(BF16)

    keep_top = jnp.where(band == 0, 0.0, 1.0)
    keep_bot = jnp.where(band == nband - 1, 0.0, 1.0)

    def receive(buf, fields, way):
        for n, a in enumerate(fields):
            value = buf[way, n].astype(F32)
            if way == 0:
                st(xf, a * AREA + (RI + 2) * XC + 8, CJ, value * keep_bot)
            elif way == 1:
                st(xf, a * AREA + XC + 8, CJ, value * keep_top)
            else:
                st(xf, a * AREA + 2 * XC + (8 + CJ if way == 2 else 7), RI, value[:RI], XC)

    for way, fields in enumerate((UP2, DOWN2, LEFT2, RIGHT2)):
        message(m_2, fields, way)
        n = len(fields)
        halo2.append(
            remote(m_2.at[way, :n], r_2.at[way, :n], hs.at[8 + way], hr.at[8 + way], near(*ways[way]))
        )
    def window(ref, a, i, dj, n):
        return jnp.concatenate(
            [ld(ref, a * AREA + (i + q + 2) * XC + 8 + dj, CJ) for q in range(n)], axis=0
        )

    def up(left, r, s):
        terms = []
        for k, di in ((1, 0),) if r == 0 else ((2, 0), (0, 1)):
            for l, dj in ((1, 0),) if s == 0 else ((2, 0), (0, 1)):
                terms.append((2 * di + dj, (3 * k + l) * CH))
        terms = [lambda n=n, at=at: dot(left[n], upw[at : at + CH, :]) for n, at in terms]
        return terms[0], sum((term() for term in terms[1:]), 0.0)

    def activate(r, s, pre):
        ph = 2 * r + s
        sig = jax.nn.sigmoid(pre)
        act = (pre * sig).astype(BF16).astype(F32)
        dfac[ph] = sig * (1.0 + pre * (1.0 - sig))
        for q in range(RI):
            st(af, ph * AREA + (q + 2) * XC + 8, CJ, act[16 * q : 16 * q + 16])
        actt[:, ph * 192 : ph * 192 + 192] = act.T.astype(BF16)

    ce[0] = window(xf, 0, 0, 0, RI).astype(BF16)
    cet[0] = window(xf, 0, 0, 0, RI).T.astype(BF16)
    for r in range(2):
        for s in range(2):
            ph = 2 * r + s
            at = (3 * (1 + r) + 1 + s) * CH
            own = dot(ce[0], upw[at : at + CH, :]) + window(xf, 1 + ph, 0, 0, RI)
            if ph:
                dfac[ph] = own
            else:
                activate(0, 0, own)
            tv[2 * ph] = window(xf, 5 + ph, -1, 0, 14).astype(BF16)
            tvp[2 * ph] = dot(tv[2 * ph], perm).astype(BF16)

    for c in halo1:
        c.wait()
    for c in halo2:
        c.start()
    for way, fields in enumerate((UP1, DOWN1, LEFT1, RIGHT1)):
        receive(r_1, fields, way)
    for m, (di, dj, fields) in enumerate(CORNERS):
        keep = keep_bot if di < 0 else keep_top
        for n, a in enumerate(fields):
            at = a * AREA + (RI + 2 if di < 0 else 1) * XC + (8 + CJ if dj < 0 else 7)
            st(xf, at, 1, r_co[m, n : n + 1] * keep)

    for n in range(1, 4):
        ce[n] = window(xf, 0, n // 2, n % 2, RI).astype(BF16)
    for r, s in ((0, 1), (1, 0), (1, 1)):
        activate(r, s, dfac[2 * r + s] + up(ce, r, s)[1])

    ends = []
    for ph in range(4):
        for i in (-1, RI):
            ends.append(window(xf, 5 + ph, i, 0, 1).astype(BF16))
            tv[2 * ph, 16 * (i + 1) : 16 * (i + 2)] = ends[-1]
    ends = dot(jnp.concatenate(ends, axis=0), perm).astype(BF16)
    for ph in range(4):
        for m, i in enumerate((-1, RI)):
            tvp[2 * ph, 16 * (i + 1) : 16 * (i + 2)] = ends[16 * (2 * ph + m) : 16 * (2 * ph + m + 1)]
        tv[2 * ph + 1] = window(xf, 5 + ph, -1, 1 if ph % 2 == 0 else -1, 14).astype(BF16)
        tvp[2 * ph + 1] = dot(tv[2 * ph + 1], perm).astype(BF16)

    def view(ref, er, es, i0, n):
        (r, di), (s, dj) = split(er), split(es)
        at = (i0 + di + 1) * 16
        return ref[(2 * r + s) * 2 + (1 if dj else 0), at : at + 16 * n]

    def put(arr, t, value):
        start = t * CH
        while start < (t + 1) * CH:
            f, off = divmod(start, FB)
            stop = min((t + 1) * CH, (f + 1) * FB)
            gsum[arr, f // (2 * Y), (f // 2) % Y, f % 2, off : off + stop - start] = value[
                start - t * CH : stop - t * CH
            ]
            start = stop

    def first(arr, a):
        c = remote(gsum.at[arr, a, :, 1 - core], r0.at[arr, a], s0s.at[arr, a], s0r.at[arr, a], at_core())
        c.start()
        return c

    step0c = []
    for t, (k, l) in enumerate(TAPS):
        right = jnp.concatenate(
            [view(tvp, r - k + 1, s - l + 1, 0, RI) for r in range(2) for s in range(2)], axis=0
        )
        put(0, t, dot(actt[...], right).astype(BF16))
        if XH == 2 and t == 6:
            step0c.append(first(0, 0))
    step0c.append(first(0, XH - 1))

    def half(x2):
        return pl.ds(pl.multiple_of(rem(x2, XL) * HL, HL), HL)

    def stage1(arr, arrived):
        steps = [[], []]
        for a in range(XH):
            arrived[a].wait()
            for b in range(Y):
                s1[arr, a, b] = gsum[arr, a, b, core] + r0[arr, a, b]
            for d in far_y:
                q = Y - d - 1
                steps[0].append(
                    remote(
                        s1.at[arr, a, rem(yy + d, Y), :RA], r1a.at[arr, q, a],
                        s1s.at[arr, a, d - 1], s1r.at[arr, a, q], at_y(d),
                    )
                )
                steps[0][-1].start()
        for d in far_x:
            q, x2 = NX - d - 1, rem(xx + d, NX)
            steps[1].append(
                remote(
                    s1.at[arr, div(x2, XL), :, RA:, half(x2)], r1b.at[arr, q],
                    s1s.at[arr, 2, d - 1], s1r.at[arr, 2, q], at_x(d),
                )
            )
            steps[1][-1].start()
        return steps

    phases = [(r, s) for r in range(2) for s in range(2)]

    def stacked(ref, step, group):
        return jnp.concatenate(
            [
                jnp.concatenate([view(ref, *step(r, s, k, l), 0, RI) for r, s in group], axis=0)
                for k, l in TAPS
            ],
            axis=1,
        )

    for g in range(0, 4, 4):
        group = phases[g : g + 4]
        left = stacked(tv, lambda r, s, k, l: (r - k + 1, s - l + 1), group)
        grads = dot(left, convwt[...])
        for n, (r, s) in enumerate(group):
            ph = 2 * r + s
            grad = (grads[192 * n : 192 * n + 192] * dfac[ph]).astype(BF16)
            gpp[ph] = dot(grad, perm).astype(BF16)
            gb[ph] = grad

    for n in range(1, 4):
        cet[n] = window(xf, 0, n // 2, n % 2, RI).T.astype(BF16)
    step1c = stage1(0, step0c)
    step0u = []
    for t, (k, l) in enumerate(TAPS):
        (r, di), (s, dj) = (((1, 1), (0, 0), (1, 0))[m] for m in (k, l))
        put(1, t, dot(cet[2 * di + dj], gpp[2 * r + s]).astype(BF16))
        if XH == 2 and t == 6:
            step0u.append(first(1, 0))
    step0u.append(first(1, XH - 1))

    def stage2a(arr, steps):
        for c in steps:
            c.wait()
        for a in range(XH):
            total = gsum[arr, a, yy, core, :RA].astype(F32) + r0[arr, a, yy, :RA].astype(F32)
            for d in range(Y - 1):
                total = total + r1a[arr, d, a].astype(F32)
            a1a[arr, a] = total
            s2a[arr, a] = total.astype(BF16)
        out = []
        for d in far_x:
            q, x2 = NX - d - 1, rem(xx + d, NX)
            out.append(
                remote(
                    s2a.at[arr, div(x2, XL), :, half(x2)], r2a.at[arr, q],
                    s2s.at[arr, 0, d - 1], s2r.at[arr, 0, q], at_x(d),
                )
            )
            out[-1].start()
        return out

    def stage2b(arr, steps):
        for c in steps:
            c.wait()
        own = half(xx)
        for b in range(Y):
            total = gsum[arr, xh, b, core, RA:, own].astype(F32) + r0[arr, xh, b, RA:, own].astype(F32)
            for d in range(NX - 1):
                total = total + r1b[arr, d, b].astype(F32)
            a1b[arr, b] = total
            s2b[arr, b] = total.astype(BF16)
        out = []
        for d in far_y:
            q = Y - d - 1
            out.append(
                remote(
                    s2b.at[arr, rem(yy + d, Y)], r2b.at[arr, q],
                    s2s.at[arr, 1, d - 1], s2r.at[arr, 1, q], at_y(d),
                )
            )
            out[-1].start()
        return out

    def stage3(arr, steps):
        for c in steps[0]:
            c.wait()
        total = a1a[arr, xh, :, half(xx)]
        for d in range(NX - 1):
            total = total + r2a[arr, d].astype(F32)
        pad[arr, :RA] = total
        for c in steps[1]:
            c.wait()
        total = a1b[arr, yy]
        for d in range(Y - 1):
            total = total + r2b[arr, d].astype(F32)
        pad[arr, RA:FB] = total
        turned = pad[arr].T
        for z in range(Z):
            a3[arr, z] = turned[z * CB : (z + 1) * CB]
            s3[arr, z] = turned[z * CB : (z + 1) * CB].astype(BF16)
        out = []
        for d in far_z:
            q = Z - d - 1
            out.append(
                remote(s3.at[arr, rem(zz + d, Z)], r3.at[arr, q], s3s.at[arr, d - 1], s3r.at[arr, q], at_z(d))
            )
            out[-1].start()
        return out

    def finish(arr, steps, out):
        for c in steps:
            c.wait()
        total = a3[arr, zz]
        for d in range(Z - 1):
            total = total + r3[arr, d].astype(F32)
        out[...] = total[:, :FB]

    def decode(group):
        outs = dot(stacked(av, lambda r, s, k, l: (r + k - 1, s + l - 1), group), convw[...])
        for n, (r, s) in enumerate(group):
            out = outs[192 * n : 192 * n + 192]
            for i in range(RI):
                st(dec_v, (2 * i + r) * 2 * CJ + s, CJ, out[16 * i : 16 * i + 16], 2)

    step1u = stage1(1, step0u)

    for c in halo2:
        c.wait()
    for way, fields in enumerate((UP2, DOWN2, LEFT2, RIGHT2)):
        receive(r_2, fields, way)

    def border(a, di, dj):
        return jnp.concatenate(
            [window(xf, a, di - 1, dj, 1), window(xf, a, di + RI, dj, 1)]
            + [rows(a, di - 1, dj - 1, 16), rows(a, di - 1, dj + CJ, 16)],
            axis=0,
        )

    for di in range(2):
        for dj in range(2):
            cg[2 * di + dj] = border(0, di, dj).astype(BF16)
    line = lax.broadcasted_iota(jnp.int32, (64, CH), 0)
    first_row = (line < 16) | ((line >= 32) & (line % 16 == 0))
    last_row = ((line >= 16) & (line < 32)) | ((line >= 32) & (line % 16 == RI + 1))
    ghost = ((band == 0) & first_row) | ((band == nband - 1) & last_row)
    for r in range(2):
        for s in range(2):
            ph = 2 * r + s
            own, others = up(cg, r, s)
            pre = own() + others + border(1 + ph, 0, 0)
            sig = jax.nn.sigmoid(pre)
            act = jnp.where(ghost, 0.0, pre * sig).astype(BF16).astype(F32)
            dghost[ph] = jnp.where(ghost, 0.0, sig * (1.0 + pre * (1.0 - sig)))
            st(af, ph * AREA + XC + 8, CJ, act[:16])
            st(af, ph * AREA + (RI + 2) * XC + 8, CJ, act[16:32])
            st(af, ph * AREA + XC + 7, 16, act[32:48], XC)
            st(af, ph * AREA + XC + 8 + CJ, 16, act[48:], XC)

    for s in range(2):
        for v, dj in enumerate((0, 1 if s == 0 else -1)):
            tv[2 * s + v, :16] = window(xf, 5 + s, -1, dj, 1).astype(BF16)

    for r in range(2):
        for s in range(2):
            for v, dj in enumerate((0, 1 if s == 0 else -1)):
                av[(2 * r + s) * 2 + v] = window(af, 2 * r + s, -1, dj, 14).astype(BF16)

    for ph in range(4):
        grad = gb[ph].astype(F32)
        for q in range(RI):
            st(gf, ph * AREA + (q + 2) * XC + 8, CJ, grad[16 * q : 16 * q + 16])
    lines, slopes = [], []
    for s in range(2):
        lines.append(jnp.concatenate([view(tv, 2 - k, s - l + 1, -1, 1) for k, l in TAPS], axis=1))
        slopes.append(dghost[2 + s, :16])
    for r in range(2):
        column = []
        for k, l in TAPS:
            (r2, di), (s2, dj) = split(r - k + 1), split(2 - l)
            column.append(rows(5 + 2 * r2 + s2, -1 + di, -1 + dj, 16).astype(BF16))
        lines.append(jnp.concatenate(column, axis=1))
        slopes.append(dghost[2 * r + 1, 32:48])
    grad = dot(jnp.concatenate(lines, axis=0), convwt[...]) * jnp.concatenate(slopes, axis=0)
    grad = grad.astype(BF16).astype(F32)
    st(gf, 2 * AREA + XC + 8, CJ, grad[:16])
    st(gf, 3 * AREA + XC + 8, CJ, grad[16:32])
    st(gf, AREA + XC + 7, 16, grad[32:48], XC)
    st(gf, 3 * AREA + XC + 7, 16, grad[48:], XC)
    for t, (k, l) in enumerate(TAPS):
        (r, di), (s, dj) = split(k - 1), split(l - 1)
        gv[:, t * CH : (t + 1) * CH] = window(gf, 2 * r + s, di, dj, RI).astype(BF16)

    decode(phases[0:4])
    gc_o[...] = dot(gv[...], upwt[...]).astype(BF16)
    for p in range(2 * RI):
        dec_o[p] = ld(dec_v, p * 2 * CJ, 2 * CJ).astype(BF16)

    step2c = [stage2a(0, step1c[0]), stage2b(0, step1c[1])]
    step2u = [stage2a(1, step1u[0]), stage2b(1, step1u[1])]
    step3c = stage3(0, step2c)
    step3u = stage3(1, step2u)
    finish(0, step3c, gw_o)
    finish(1, step3u, gu_o)


def deliver(*refs):
    n = (len(refs) - 1) // 2
    copies = [pltpu.make_async_copy(refs[i], refs[n + i], refs[-1].at[i]) for i in range(n)]
    for c in copies:
        c.start()
    for c in copies:
        c.wait()


def local(dims, coarse, skip, up_weight, conv_weight, cotangent):
    XH, Y, Z, XL = dims
    NX, HL = XH * XL, CH // XL
    FB, CB = 9 * CH // (XH * Y * 2), CH // (Z * XL)
    RA = FB // 16 * 5 // 9 * 16
    RB = FB - RA
    FP = -(-FB // 128) * 128
    hbm, vmem = pl.BlockSpec(memory_space=pltpu.HBM), pl.BlockSpec(memory_space=pltpu.VMEM)
    V, dma = pltpu.VMEM, pltpu.SemaphoreType.DMA
    wide = V((9 * CH, CH), BF16)
    scratch = [
        V((RI, CJ, CH), BF16), V((2 * RI, 2 * CJ, CH), BF16), V((2 * RI, 2 * CJ, CH), BF16),
        wide, wide, wide, wide,
        V((2, 9 * AREA, 128), F32), V((2, 4 * CJ, 128), F32), V((2, 4 * CJ, 128), F32),
        V((2, 4 * AREA, 128), F32), V((2, 4 * AREA, 128), F32), V((4, 192, CH), F32), V((4, 64, CH), F32),
        V((4, 192, CH), BF16), V((4, 64, CH), BF16), V((4, CH, 192), BF16), V((4, 192, CH), BF16), V((4, 192, CH), BF16),
        V((8, 224, CH), BF16), V((8, 224, CH), BF16), V((8, 224, CH), BF16),
        V((192, 9 * CH), BF16), V((CH, 768), BF16), V((2, 4 * RI * CJ, 128), F32),
        V((4, 3, 16, CH), BF16), V((4, 5, 16, CH), BF16), V((4, 8, CH), F32),
        V((4, 3, 16, CH), BF16), V((4, 5, 16, CH), BF16), V((4, 8, CH), F32),
        V((2, XH, Y, 2, FB, CH), BF16), V((2, XH, Y, FB, CH), BF16), V((2, XH, Y, FB, CH), BF16),
        V((2, Y - 1, XH, RA, CH), BF16), V((2, NX - 1, Y, RB, HL), BF16),
        V((2, XH, RA, CH), F32), V((2, Y, RB, HL), F32), V((2, XH, RA, CH), BF16), V((2, Y, RB, HL), BF16),
        V((2, NX - 1, RA, HL), BF16), V((2, Y - 1, RB, HL), BF16),
        V((2, FP, HL), F32), V((2, Z, CB, FP), F32), V((2, Z, CB, FP), BF16), V((2, Z - 1, CB, FP), BF16),
        dma((5,)), dma((12,)), dma((12,)), dma((2, 2)), dma((2, 2)),
        dma((2, 3, 3)), dma((2, 3, 3)), dma((2, 2, 3)), dma((2, 2, 3)), dma((2, Z - 1)), dma((2, Z - 1)),
    ]
    shapes = (
        jax.ShapeDtypeStruct((2 * RI, 2 * CJ, CH), BF16),
        jax.ShapeDtypeStruct((RI * CJ, CH), BF16),
        jax.ShapeDtypeStruct((CB, FB), F32),
        jax.ShapeDtypeStruct((CB, FB), F32),
    )
    inputs = (coarse, skip, up_weight.reshape(9 * CH, CH), conv_weight.reshape(9 * CH, CH), cotangent)
    inputs = [pltpu.with_memory_space_constraint(x, pltpu.HBM) for x in inputs]
    results = pl.pallas_call(
        functools.partial(kernel, dims),
        out_shape=shapes,
        in_specs=[hbm] * 5,
        out_specs=(vmem,) * 4,
        scratch_shapes=scratch,
        compiler_params=pltpu.CompilerParams(
            collective_id=0, has_side_effects=True, vmem_limit_bytes=36 * 2**20
        ),
    )(*inputs)
    decoded, grad_coarse, grad_up, grad_conv = pl.pallas_call(
        deliver,
        out_shape=shapes,
        in_specs=[vmem] * 4,
        out_specs=(hbm,) * 4,
        scratch_shapes=[dma((4,))],
        compiler_params=pltpu.CompilerParams(vmem_limit_bytes=4 * 2**20),
    )(*results)
    return decoded, grad_coarse.reshape(RI, CJ, CH), grad_up.T, grad_conv.T


def build(mesh, dims):
    cells = P("band", "face", None)
    return jax.shard_map(
        functools.partial(local, dims),
        mesh=mesh,
        in_specs=(cells, cells, P(), P(), cells),
        out_specs=(cells, cells, P("face", "band"), P("face", "band")),
        check_vma=False,
    )


def solution(mesh):
    return build(mesh, (2, 4, 8, 2))
```

```python
import functools

import jax
import jax.numpy as jnp
from jax import lax
from jax.experimental import pallas as pl
from jax.experimental.pallas import tpu as pltpu
from jax.sharding import PartitionSpec as P

F32, BF16 = jnp.float32, jnp.bfloat16
MESH = pl.DeviceIdType.MESH
CH = 256
RI, CJ = 12, 16
XR, XC = 18, 32
AREA = XR * XC

UP1, UP2 = (0, 5, 6), (1, 2)
DOWN1, DOWN2 = (7, 8), (0, 3, 4, 5, 6)
LEFT1, LEFT2 = (0, 5, 7), (1, 3)
RIGHT1, RIGHT2 = (6, 8), (0, 2, 4, 5, 7)
CORNERS = (
    (-1, -1, (0, 1, 5)),
    (-1, 1, (0, 2, 5, 6)),
    (1, -1, (0, 3, 5, 7)),
    (1, 1, (0, 4, 5, 6, 7, 8)),
)
TAPS = [(k, l) for k in range(3) for l in range(3)]


def split(e):
    return e % 2, e // 2


def dot(a, b):
    return jnp.dot(a, b, preferred_element_type=F32)


def ld(ref, at, n, stride=1):
    if stride == 1:
        return jnp.concatenate([ref[h, pl.ds(at, n), :] for h in range(2)], axis=-1)
    return jnp.concatenate([ref[h, pl.ds(at, n, stride=stride), :] for h in range(2)], axis=-1)


def st(ref, at, n, value, stride=1):
    for h in range(2):
        part = value[:, 128 * h : 128 * h + 128]
        if stride == 1:
            ref[h, pl.ds(at, n), :] = part
        else:
            ref[h, pl.ds(at, n, stride=stride), :] = part


def far(n):
    return sorted(range(1, n), key=lambda d: (-min(d, n - d), d))


def kernel(
    dims,
    coarse_h, skip_h, upw_h, convw_h, cot_h,
    dec_o, gc_o, gu_o, gw_o,
    coarse_v, skip_v, cot_v, upw, convw, upwt, convwt,
    xf, fs, ft, af, gf, dfac, dghost, ce, cg, cet, gpp, gb, tv, tvp, av, gv, actt, dec_v,
    m_1, m_2, m_co, r_1, r_2, r_co,
    gsum, r0, s1, r1a, r1b, a1a, a1b, s2a, s2b, r2a, r2b, pad, a3, s3, r3,
    in_sem, hs, hr, s0s, s0r, s1s, s1r, s2s, s2r, s3s, s3r,
):
    loads = [
        pltpu.make_async_copy(src, dst, in_sem.at[n])
        for n, (src, dst) in enumerate(
            ((coarse_h, coarse_v), (cot_h, cot_v), (skip_h, skip_v), (convw_h, convw), (upw_h, upw))
        )
    ]
    for c in loads:
        c.start()

    XH, Y, Z, XL = dims
    NX = XH * XL
    HL = CH // XL
    FB = 9 * CH // (XH * Y * 2)
    RA = FB // 16 * 6 // 9 * 16
    CB = CH // (Z * XL)
    nface, nband = XH * Y * 2, Z * XL
    face, band = lax.axis_index("face"), lax.axis_index("band")
    rem, div = lax.rem, lax.div
    core = rem(face, 2)
    yy = rem(div(face, 2), Y)
    xh = div(face, 2 * Y)
    xl = rem(band, XL)
    zz = div(band, XL)
    xx = xh * XL + xl

    def dev(xx_, yy_, core_, zz_):
        return {
            "face": div(xx_, XL) * (2 * Y) + yy_ * 2 + core_,
            "band": zz_ * XL + rem(xx_, XL),
        }

    def near(di, dj):
        return {"face": rem(face + dj + nface, nface), "band": rem(band + di + nband, nband)}

    def at_core():
        return dev(xx, yy, 1 - core, zz)

    def at_y(d):
        return dev(xx, rem(yy + d, Y), core, zz)

    def at_x(d):
        return dev(rem(xx + d, NX), yy, core, zz)

    def at_z(d):
        return dev(xx, yy, core, rem(zz + d, Z))

    ways = [(-1, 0), (1, 0), (0, -1), (0, 1), (-1, -1), (-1, 1), (1, -1), (1, 1)]
    far_z, far_y, far_x = far(Z), far(Y), far(NX)
    partners = [near(*w) for w in ways[4:]] + [at_z(d) for d in far_z]
    partners += [at_x(d) for d in far_x] + [at_y(d) for d in far_y]
    partners += [near(*w) for w in ways[:4]] + [at_core()]
    barrier = pltpu.get_barrier_semaphore()
    for p in partners:
        pl.semaphore_signal(barrier, inc=1, device_id=p, device_id_type=MESH)

    def rows(a, i, col, n):
        return ld(xf, a * AREA + (i + 2) * XC + 8 + col, n, XC)

    for c in loads[:3]:
        c.wait()

    def spread(i, carry):
        base = pl.multiple_of((i + 2) * XC + 8, 8)
        st(xf, base, CJ, coarse_v[i].astype(F32))
        for src, stage, first in ((skip_v, fs, 1), (cot_v, ft, 5)):
            for r in range(2):
                st(stage, r * 2 * CJ, 2 * CJ, src[2 * i + r].astype(F32))
            for r in range(2):
                for s in range(2):
                    part = ld(stage, r * 2 * CJ + s, CJ, 2)
                    st(xf, pl.multiple_of(base + (first + 2 * r + s) * AREA, 8), CJ, part)
        return carry

    lax.fori_loop(0, RI, spread, 0)

    def message(buf, fields, way):
        for n, a in enumerate(fields):
            if way < 2:
                buf[way, n] = ld(xf, a * AREA + (2 if way == 0 else RI + 1) * XC + 8, CJ).astype(BF16)
            else:
                buf[way, n] = rows(a, 0, 0 if way == 2 else CJ - 1, 16).astype(BF16)

    for way, fields in enumerate((UP1, DOWN1, LEFT1, RIGHT1)):
        message(m_1, fields, way)
    for m, (di, dj, fields) in enumerate(CORNERS):
        for n, a in enumerate(fields):
            at = a * AREA + (2 + (0 if di < 0 else RI - 1)) * XC + 8 + (0 if dj < 0 else CJ - 1)
            m_co[m, n : n + 1] = ld(xf, at, 1)

    pl.semaphore_wait(barrier, len(partners))

    def remote(src, dst, ssem, rsem, to):
        return pltpu.make_async_remote_copy(
            src_ref=src, dst_ref=dst, send_sem=ssem, recv_sem=rsem, device_id=to, device_id_type=MESH
        )

    halo1, halo2 = [], []
    for m, (di, dj, _) in enumerate(CORNERS):
        halo1.append(remote(m_co.at[m], r_co.at[m], hs.at[m], hr.at[m], near(di, dj)))
    for way, fields in enumerate((UP1, DOWN1, LEFT1, RIGHT1)):
        n = len(fields)
        halo1.append(
            remote(m_1.at[way, :n], r_1.at[way, :n], hs.at[4 + way], hr.at[4 + way], near(*ways[way]))
        )
    for c in halo1:
        c.start()
    for c in loads[3:]:
        c.wait()

    def turn(t, carry):
        at = pl.multiple_of(t * CH, CH)
        convwt[pl.ds(at, CH), :] = convw[pl.ds(at, CH), :].T
        upwt[pl.ds(at, CH), :] = upw[pl.ds(at, CH), :].T
        return carry

    lax.fori_loop(0, 9, turn, 0)
    src = lax.broadcasted_iota(jnp.int32, (CH, CH), 0)
    dst = lax.broadcasted_iota(jnp.int32, (CH, CH), 1)
    wanted = (((dst % HL) // CB) * XL + dst // HL) * CB + dst % CB
    perm = jnp.where(src == wanted, 1.0, 0.0).astype(BF16)

    keep_top = jnp.where(band == 0, 0.0, 1.0)
    keep_bot = jnp.where(band == nband - 1, 0.0, 1.0)

    def receive(buf, fields, way):
        for n, a in enumerate(fields):
            value = buf[way, n].astype(F32)
            if way == 0:
                st(xf, a * AREA + (RI + 2) * XC + 8, CJ, value * keep_bot)
            elif way == 1:
                st(xf, a * AREA + XC + 8, CJ, value * keep_top)
            else:
                st(xf, a * AREA + 2 * XC + (8 + CJ if way == 2 else 7), RI, value[:RI], XC)

    for way, fields in enumerate((UP2, DOWN2, LEFT2, RIGHT2)):
        message(m_2, fields, way)
        n = len(fields)
        halo2.append(
            remote(m_2.at[way, :n], r_2.at[way, :n], hs.at[8 + way], hr.at[8 + way], near(*ways[way]))
        )
    def window(ref, a, i, dj, n):
        return jnp.concatenate(
            [ld(ref, a * AREA + (i + q + 2) * XC + 8 + dj, CJ) for q in range(n)], axis=0
        )

    def up(left, r, s):
        terms = []
        for k, di in ((1, 0),) if r == 0 else ((2, 0), (0, 1)):
            for l, dj in ((1, 0),) if s == 0 else ((2, 0), (0, 1)):
                terms.append((2 * di + dj, (3 * k + l) * CH))
        terms = [lambda n=n, at=at: dot(left[n], upw[at : at + CH, :]) for n, at in terms]
        return terms[0], sum((term() for term in terms[1:]), 0.0)

    def activate(r, s, pre):
        ph = 2 * r + s
        sig = jax.nn.sigmoid(pre)
        act = (pre * sig).astype(BF16).astype(F32)
        dfac[ph] = sig * (1.0 + pre * (1.0 - sig))
        for q in range(RI):
            st(af, ph * AREA + (q + 2) * XC + 8, CJ, act[16 * q : 16 * q + 16])
        actt[:, ph * 192 : ph * 192 + 192] = act.T.astype(BF16)

    ce[0] = window(xf, 0, 0, 0, RI).astype(BF16)
    cet[0] = window(xf, 0, 0, 0, RI).T.astype(BF16)
    for r in range(2):
        for s in range(2):
            ph = 2 * r + s
            at = (3 * (1 + r) + 1 + s) * CH
            own = dot(ce[0], upw[at : at + CH, :]) + window(xf, 1 + ph, 0, 0, RI)
            if ph:
                dfac[ph] = own
            else:
                activate(0, 0, own)
            tv[2 * ph] = window(xf, 5 + ph, -1, 0, 14).astype(BF16)
            tvp[2 * ph] = dot(tv[2 * ph], perm).astype(BF16)

    for c in halo1:
        c.wait()
    for c in halo2:
        c.start()
    for way, fields in enumerate((UP1, DOWN1, LEFT1, RIGHT1)):
        receive(r_1, fields, way)
    for m, (di, dj, fields) in enumerate(CORNERS):
        keep = keep_bot if di < 0 else keep_top
        for n, a in enumerate(fields):
            at = a * AREA + (RI + 2 if di < 0 else 1) * XC + (8 + CJ if dj < 0 else 7)
            st(xf, at, 1, r_co[m, n : n + 1] * keep)

    for n in range(1, 4):
        ce[n] = window(xf, 0, n // 2, n % 2, RI).astype(BF16)
    for r, s in ((0, 1), (1, 0), (1, 1)):
        activate(r, s, dfac[2 * r + s] + up(ce, r, s)[1])

    ends = []
    for ph in range(4):
        for i in (-1, RI):
            ends.append(window(xf, 5 + ph, i, 0, 1).astype(BF16))
            tv[2 * ph, 16 * (i + 1) : 16 * (i + 2)] = ends[-1]
    ends = dot(jnp.concatenate(ends, axis=0), perm).astype(BF16)
    for ph in range(4):
        for m, i in enumerate((-1, RI)):
            tvp[2 * ph, 16 * (i + 1) : 16 * (i + 2)] = ends[16 * (2 * ph + m) : 16 * (2 * ph + m + 1)]
        tv[2 * ph + 1] = window(xf, 5 + ph, -1, 1 if ph % 2 == 0 else -1, 14).astype(BF16)
        tvp[2 * ph + 1] = dot(tv[2 * ph + 1], perm).astype(BF16)

    def view(ref, er, es, i0, n):
        (r, di), (s, dj) = split(er), split(es)
        at = (i0 + di + 1) * 16
        return ref[(2 * r + s) * 2 + (1 if dj else 0), at : at + 16 * n]

    def put(arr, t, value):
        start = t * CH
        while start < (t + 1) * CH:
            f, off = divmod(start, FB)
            stop = min((t + 1) * CH, (f + 1) * FB)
            gsum[arr, f // (2 * Y), (f // 2) % Y, f % 2, off : off + stop - start] = value[
                start - t * CH : stop - t * CH
            ]
            start = stop

    def first(arr, a):
        c = remote(gsum.at[arr, a, :, 1 - core], r0.at[arr, a], s0s.at[arr, a], s0r.at[arr, a], at_core())
        c.start()
        return c

    step0c = []
    for t, (k, l) in enumerate(TAPS):
        right = jnp.concatenate(
            [view(tvp, r - k + 1, s - l + 1, 0, RI) for r in range(2) for s in range(2)], axis=0
        )
        put(0, t, dot(actt[...], right).astype(BF16))
        if XH == 2 and t == 6:
            step0c.append(first(0, 0))
    step0c.append(first(0, XH - 1))

    def half(x2):
        return pl.ds(pl.multiple_of(rem(x2, XL) * HL, HL), HL)

    def stage1(arr, arrived):
        steps = [[], []]
        for a in range(XH):
            arrived[a].wait()
            for b in range(Y):
                s1[arr, a, b] = gsum[arr, a, b, core] + r0[arr, a, b]
            for d in far_y:
                q = Y - d - 1
                steps[0].append(
                    remote(
                        s1.at[arr, a, rem(yy + d, Y), :RA], r1a.at[arr, q, a],
                        s1s.at[arr, a, d - 1], s1r.at[arr, a, q], at_y(d),
                    )
                )
                steps[0][-1].start()
        for d in far_x:
            q, x2 = NX - d - 1, rem(xx + d, NX)
            steps[1].append(
                remote(
                    s1.at[arr, div(x2, XL), :, RA:, half(x2)], r1b.at[arr, q],
                    s1s.at[arr, 2, d - 1], s1r.at[arr, 2, q], at_x(d),
                )
            )
            steps[1][-1].start()
        return steps

    phases = [(r, s) for r in range(2) for s in range(2)]

    def stacked(ref, step, group):
        return jnp.concatenate(
            [
                jnp.concatenate([view(ref, *step(r, s, k, l), 0, RI) for r, s in group], axis=0)
                for k, l in TAPS
            ],
            axis=1,
        )

    for g in range(0, 4, 4):
        group = phases[g : g + 4]
        left = stacked(tv, lambda r, s, k, l: (r - k + 1, s - l + 1), group)
        grads = dot(left, convwt[...])
        for n, (r, s) in enumerate(group):
            ph = 2 * r + s
            grad = (grads[192 * n : 192 * n + 192] * dfac[ph]).astype(BF16)
            gpp[ph] = dot(grad, perm).astype(BF16)
            gb[ph] = grad

    for n in range(1, 4):
        cet[n] = window(xf, 0, n // 2, n % 2, RI).T.astype(BF16)
    step1c = stage1(0, step0c)
    step0u = []
    for t, (k, l) in enumerate(TAPS):
        (r, di), (s, dj) = (((1, 1), (0, 0), (1, 0))[m] for m in (k, l))
        put(1, t, dot(cet[2 * di + dj], gpp[2 * r + s]).astype(BF16))
        if XH == 2 and t == 6:
            step0u.append(first(1, 0))
    step0u.append(first(1, XH - 1))

    def stage2a(arr, steps):
        for c in steps:
            c.wait()
        for a in range(XH):
            total = gsum[arr, a, yy, core, :RA].astype(F32) + r0[arr, a, yy, :RA].astype(F32)
            for d in range(Y - 1):
                total = total + r1a[arr, d, a].astype(F32)
            a1a[arr, a] = total
            s2a[arr, a] = total.astype(BF16)
        out = []
        for d in far_x:
            q, x2 = NX - d - 1, rem(xx + d, NX)
            out.append(
                remote(
                    s2a.at[arr, div(x2, XL), :, half(x2)], r2a.at[arr, q],
                    s2s.at[arr, 0, d - 1], s2r.at[arr, 0, q], at_x(d),
                )
            )
            out[-1].start()
        return out

    def stage2b(arr, steps):
        for c in steps:
            c.wait()
        own = half(xx)
        for b in range(Y):
            total = gsum[arr, xh, b, core, RA:, own].astype(F32) + r0[arr, xh, b, RA:, own].astype(F32)
            for d in range(NX - 1):
                total = total + r1b[arr, d, b].astype(F32)
            a1b[arr, b] = total
            s2b[arr, b] = total.astype(BF16)
        out = []
        for d in far_y:
            q = Y - d - 1
            out.append(
                remote(
                    s2b.at[arr, rem(yy + d, Y)], r2b.at[arr, q],
                    s2s.at[arr, 1, d - 1], s2r.at[arr, 1, q], at_y(d),
                )
            )
            out[-1].start()
        return out

    def stage3(arr, steps):
        for c in steps[0]:
            c.wait()
        total = a1a[arr, xh, :, half(xx)]
        for d in range(NX - 1):
            total = total + r2a[arr, d].astype(F32)
        pad[arr, :RA] = total
        for c in steps[1]:
            c.wait()
        total = a1b[arr, yy]
        for d in range(Y - 1):
            total = total + r2b[arr, d].astype(F32)
        pad[arr, RA:FB] = total
        turned = pad[arr].T
        for z in range(Z):
            a3[arr, z] = turned[z * CB : (z + 1) * CB]
            s3[arr, z] = turned[z * CB : (z + 1) * CB].astype(BF16)
        out = []
        for d in far_z:
            q = Z - d - 1
            out.append(
                remote(s3.at[arr, rem(zz + d, Z)], r3.at[arr, q], s3s.at[arr, d - 1], s3r.at[arr, q], at_z(d))
            )
            out[-1].start()
        return out

    def finish(arr, steps, out):
        for c in steps:
            c.wait()
        total = a3[arr, zz]
        for d in range(Z - 1):
            total = total + r3[arr, d].astype(F32)
        out[...] = total[:, :FB]

    def decode(group):
        outs = dot(stacked(av, lambda r, s, k, l: (r + k - 1, s + l - 1), group), convw[...])
        for n, (r, s) in enumerate(group):
            out = outs[192 * n : 192 * n + 192]
            for i in range(RI):
                st(dec_v, (2 * i + r) * 2 * CJ + s, CJ, out[16 * i : 16 * i + 16], 2)

    step1u = stage1(1, step0u)

    for c in halo2:
        c.wait()
    for way, fields in enumerate((UP2, DOWN2, LEFT2, RIGHT2)):
        receive(r_2, fields, way)

    def border(a, di, dj):
        return jnp.concatenate(
            [window(xf, a, di - 1, dj, 1), window(xf, a, di + RI, dj, 1)]
            + [rows(a, di - 1, dj - 1, 16), rows(a, di - 1, dj + CJ, 16)],
            axis=0,
        )

    for di in range(2):
        for dj in range(2):
            cg[2 * di + dj] = border(0, di, dj).astype(BF16)
    line = lax.broadcasted_iota(jnp.int32, (64, CH), 0)
    first_row = (line < 16) | ((line >= 32) & (line % 16 == 0))
    last_row = ((line >= 16) & (line < 32)) | ((line >= 32) & (line % 16 == RI + 1))
    ghost = ((band == 0) & first_row) | ((band == nband - 1) & last_row)
    for r in range(2):
        for s in range(2):
            ph = 2 * r + s
            own, others = up(cg, r, s)
            pre = own() + others + border(1 + ph, 0, 0)
            sig = jax.nn.sigmoid(pre)
            act = jnp.where(ghost, 0.0, pre * sig).astype(BF16).astype(F32)
            dghost[ph] = jnp.where(ghost, 0.0, sig * (1.0 + pre * (1.0 - sig)))
            st(af, ph * AREA + XC + 8, CJ, act[:16])
            st(af, ph * AREA + (RI + 2) * XC + 8, CJ, act[16:32])
            st(af, ph * AREA + XC + 7, 16, act[32:48], XC)
            st(af, ph * AREA + XC + 8 + CJ, 16, act[48:], XC)

    for s in range(2):
        for v, dj in enumerate((0, 1 if s == 0 else -1)):
            tv[2 * s + v, :16] = window(xf, 5 + s, -1, dj, 1).astype(BF16)

    for r in range(2):
        for s in range(2):
            for v, dj in enumerate((0, 1 if s == 0 else -1)):
                av[(2 * r + s) * 2 + v] = window(af, 2 * r + s, -1, dj, 14).astype(BF16)

    for ph in range(4):
        grad = gb[ph].astype(F32)
        for q in range(RI):
            st(gf, ph * AREA + (q + 2) * XC + 8, CJ, grad[16 * q : 16 * q + 16])
    lines, slopes = [], []
    for s in range(2):
        lines.append(jnp.concatenate([view(tv, 2 - k, s - l + 1, -1, 1) for k, l in TAPS], axis=1))
        slopes.append(dghost[2 + s, :16])
    for r in range(2):
        column = []
        for k, l in TAPS:
            (r2, di), (s2, dj) = split(r - k + 1), split(2 - l)
            column.append(rows(5 + 2 * r2 + s2, -1 + di, -1 + dj, 16).astype(BF16))
        lines.append(jnp.concatenate(column, axis=1))
        slopes.append(dghost[2 * r + 1, 32:48])
    grad = dot(jnp.concatenate(lines, axis=0), convwt[...]) * jnp.concatenate(slopes, axis=0)
    grad = grad.astype(BF16).astype(F32)
    st(gf, 2 * AREA + XC + 8, CJ, grad[:16])
    st(gf, 3 * AREA + XC + 8, CJ, grad[16:32])
    st(gf, AREA + XC + 7, 16, grad[32:48], XC)
    st(gf, 3 * AREA + XC + 7, 16, grad[48:], XC)
    for t, (k, l) in enumerate(TAPS):
        (r, di), (s, dj) = split(k - 1), split(l - 1)
        gv[:, t * CH : (t + 1) * CH] = window(gf, 2 * r + s, di, dj, RI).astype(BF16)

    decode(phases[0:4])
    gc_o[...] = dot(gv[...], upwt[...]).astype(BF16)
    for p in range(2 * RI):
        dec_o[p] = ld(dec_v, p * 2 * CJ, 2 * CJ).astype(BF16)

    step2c = [stage2a(0, step1c[0]), stage2b(0, step1c[1])]
    step2u = [stage2a(1, step1u[0]), stage2b(1, step1u[1])]
    step3c = stage3(0, step2c)
    step3u = stage3(1, step2u)
    finish(0, step3c, gw_o)
    finish(1, step3u, gu_o)


def deliver(*refs):
    n = (len(refs) - 1) // 2
    copies = [pltpu.make_async_copy(refs[i], refs[n + i], refs[-1].at[i]) for i in range(n)]
    for c in copies:
        c.start()
    for c in copies:
        c.wait()


def local(dims, coarse, skip, up_weight, conv_weight, cotangent):
    XH, Y, Z, XL = dims
    NX, HL = XH * XL, CH // XL
    FB, CB = 9 * CH // (XH * Y * 2), CH // (Z * XL)
    RA = FB // 16 * 6 // 9 * 16
    RB = FB - RA
    FP = -(-FB // 128) * 128
    hbm, vmem = pl.BlockSpec(memory_space=pltpu.HBM), pl.BlockSpec(memory_space=pltpu.VMEM)
    V, dma = pltpu.VMEM, pltpu.SemaphoreType.DMA
    wide = V((9 * CH, CH), BF16)
    scratch = [
        V((RI, CJ, CH), BF16), V((2 * RI, 2 * CJ, CH), BF16), V((2 * RI, 2 * CJ, CH), BF16),
        wide, wide, wide, wide,
        V((2, 9 * AREA, 128), F32), V((2, 4 * CJ, 128), F32), V((2, 4 * CJ, 128), F32),
        V((2, 4 * AREA, 128), F32), V((2, 4 * AREA, 128), F32), V((4, 192, CH), F32), V((4, 64, CH), F32),
        V((4, 192, CH), BF16), V((4, 64, CH), BF16), V((4, CH, 192), BF16), V((4, 192, CH), BF16), V((4, 192, CH), BF16),
        V((8, 224, CH), BF16), V((8, 224, CH), BF16), V((8, 224, CH), BF16),
        V((192, 9 * CH), BF16), V((CH, 768), BF16), V((2, 4 * RI * CJ, 128), F32),
        V((4, 3, 16, CH), BF16), V((4, 5, 16, CH), BF16), V((4, 8, CH), F32),
        V((4, 3, 16, CH), BF16), V((4, 5, 16, CH), BF16), V((4, 8, CH), F32),
        V((2, XH, Y, 2, FB, CH), BF16), V((2, XH, Y, FB, CH), BF16), V((2, XH, Y, FB, CH), BF16),
        V((2, Y - 1, XH, RA, CH), BF16), V((2, NX - 1, Y, RB, HL), BF16),
        V((2, XH, RA, CH), F32), V((2, Y, RB, HL), F32), V((2, XH, RA, CH), BF16), V((2, Y, RB, HL), BF16),
        V((2, NX - 1, RA, HL), BF16), V((2, Y - 1, RB, HL), BF16),
        V((2, FP, HL), F32), V((2, Z, CB, FP), F32), V((2, Z, CB, FP), BF16), V((2, Z - 1, CB, FP), BF16),
        dma((5,)), dma((12,)), dma((12,)), dma((2, 2)), dma((2, 2)),
        dma((2, 3, 3)), dma((2, 3, 3)), dma((2, 2, 3)), dma((2, 2, 3)), dma((2, Z - 1)), dma((2, Z - 1)),
    ]
    shapes = (
        jax.ShapeDtypeStruct((2 * RI, 2 * CJ, CH), BF16),
        jax.ShapeDtypeStruct((RI * CJ, CH), BF16),
        jax.ShapeDtypeStruct((CB, FB), F32),
        jax.ShapeDtypeStruct((CB, FB), F32),
    )
    inputs = (coarse, skip, up_weight.reshape(9 * CH, CH), conv_weight.reshape(9 * CH, CH), cotangent)
    inputs = [pltpu.with_memory_space_constraint(x, pltpu.HBM) for x in inputs]
    results = pl.pallas_call(
        functools.partial(kernel, dims),
        out_shape=shapes,
        in_specs=[hbm] * 5,
        out_specs=(vmem,) * 4,
        scratch_shapes=scratch,
        compiler_params=pltpu.CompilerParams(
            collective_id=0, has_side_effects=True, vmem_limit_bytes=36 * 2**20
        ),
    )(*inputs)
    decoded, grad_coarse, grad_up, grad_conv = pl.pallas_call(
        deliver,
        out_shape=shapes,
        in_specs=[vmem] * 4,
        out_specs=(hbm,) * 4,
        scratch_shapes=[dma((4,))],
        compiler_params=pltpu.CompilerParams(vmem_limit_bytes=4 * 2**20),
    )(*results)
    return decoded, grad_coarse.reshape(RI, CJ, CH), grad_up.T, grad_conv.T


def build(mesh, dims):
    cells = P("band", "face", None)
    return jax.shard_map(
        functools.partial(local, dims),
        mesh=mesh,
        in_specs=(cells, cells, P(), P(), cells),
        out_specs=(cells, cells, P("face", "band"), P("face", "band")),
        check_vma=False,
    )


def solution(mesh):
    return build(mesh, (2, 4, 8, 2))
```

```python
import functools

import jax
import jax.numpy as jnp
from jax import lax
from jax.experimental import pallas as pl
from jax.experimental.pallas import tpu as pltpu
from jax.sharding import PartitionSpec as P

F32, BF16 = jnp.float32, jnp.bfloat16
MESH = pl.DeviceIdType.MESH
CH = 256
RI, CJ = 12, 16
XR, XC = 18, 32
AREA = XR * XC

UP1, UP2 = (0, 5, 6), (1, 2)
DOWN1, DOWN2 = (7, 8), (0, 3, 4, 5, 6)
LEFT1, LEFT2 = (0, 5, 7), (1, 3)
RIGHT1, RIGHT2 = (6, 8), (0, 2, 4, 5, 7)
CORNERS = (
    (-1, -1, (0, 1, 5)),
    (-1, 1, (0, 2, 5, 6)),
    (1, -1, (0, 3, 5, 7)),
    (1, 1, (0, 4, 5, 6, 7, 8)),
)
TAPS = [(k, l) for k in range(3) for l in range(3)]


def split(e):
    return e % 2, e // 2


def dot(a, b):
    return jnp.dot(a, b, preferred_element_type=F32)


def ld(ref, at, n, stride=1):
    if stride == 1:
        return jnp.concatenate([ref[h, pl.ds(at, n), :] for h in range(2)], axis=-1)
    return jnp.concatenate([ref[h, pl.ds(at, n, stride=stride), :] for h in range(2)], axis=-1)


def st(ref, at, n, value, stride=1):
    for h in range(2):
        part = value[:, 128 * h : 128 * h + 128]
        if stride == 1:
            ref[h, pl.ds(at, n), :] = part
        else:
            ref[h, pl.ds(at, n, stride=stride), :] = part


def far(n):
    return sorted(range(1, n), key=lambda d: (-min(d, n - d), d))


def kernel(
    dims,
    coarse_h, skip_h, upw_h, convw_h, cot_h,
    dec_o, gc_o, gu_o, gw_o,
    coarse_v, skip_v, cot_v, upw, convw, upwt, convwt,
    xf, fs, ft, af, gf, dfac, dghost, ce, cg, cet, gpp, gb, tv, tvp, av, gv, actt, dec_v,
    m_1, m_2, m_co, r_1, r_2, r_co,
    gsum, r0, s1, r1a, r1b, a1a, a1b, s2a, s2b, r2a, r2b, pad, a3, s3, r3,
    in_sem, hs, hr, s0s, s0r, s1s, s1r, s2s, s2r, s3s, s3r,
):
    loads = [
        pltpu.make_async_copy(src, dst, in_sem.at[n])
        for n, (src, dst) in enumerate(
            ((coarse_h, coarse_v), (cot_h, cot_v), (skip_h, skip_v), (convw_h, convw), (upw_h, upw))
        )
    ]
    for c in loads:
        c.start()

    XH, Y, Z, XL = dims
    NX = XH * XL
    HL = CH // XL
    FB = 9 * CH // (XH * Y * 2)
    RA = FB // 16 * 4 // 9 * 16
    CB = CH // (Z * XL)
    nface, nband = XH * Y * 2, Z * XL
    face, band = lax.axis_index("face"), lax.axis_index("band")
    rem, div = lax.rem, lax.div
    core = rem(face, 2)
    yy = rem(div(face, 2), Y)
    xh = div(face, 2 * Y)
    xl = rem(band, XL)
    zz = div(band, XL)
    xx = xh * XL + xl

    def dev(xx_, yy_, core_, zz_):
        return {
            "face": div(xx_, XL) * (2 * Y) + yy_ * 2 + core_,
            "band": zz_ * XL + rem(xx_, XL),
        }

    def near(di, dj):
        return {"face": rem(face + dj + nface, nface), "band": rem(band + di + nband, nband)}

    def at_core():
        return dev(xx, yy, 1 - core, zz)

    def at_y(d):
        return dev(xx, rem(yy + d, Y), core, zz)

    def at_x(d):
        return dev(rem(xx + d, NX), yy, core, zz)

    def at_z(d):
        return dev(xx, yy, core, rem(zz + d, Z))

    ways = [(-1, 0), (1, 0), (0, -1), (0, 1), (-1, -1), (-1, 1), (1, -1), (1, 1)]
    far_z, far_y, far_x = far(Z), far(Y), far(NX)
    partners = [near(*w) for w in ways[4:]] + [at_z(d) for d in far_z]
    partners += [at_x(d) for d in far_x] + [at_y(d) for d in far_y]
    partners += [near(*w) for w in ways[:4]] + [at_core()]
    barrier = pltpu.get_barrier_semaphore()
    for p in partners:
        pl.semaphore_signal(barrier, inc=1, device_id=p, device_id_type=MESH)

    def rows(a, i, col, n):
        return ld(xf, a * AREA + (i + 2) * XC + 8 + col, n, XC)

    for c in loads[:3]:
        c.wait()

    def spread(i, carry):
        base = pl.multiple_of((i + 2) * XC + 8, 8)
        st(xf, base, CJ, coarse_v[i].astype(F32))
        for src, stage, first in ((skip_v, fs, 1), (cot_v, ft, 5)):
            for r in range(2):
                st(stage, r * 2 * CJ, 2 * CJ, src[2 * i + r].astype(F32))
            for r in range(2):
                for s in range(2):
                    part = ld(stage, r * 2 * CJ + s, CJ, 2)
                    st(xf, pl.multiple_of(base + (first + 2 * r + s) * AREA, 8), CJ, part)
        return carry

    lax.fori_loop(0, RI, spread, 0)

    def message(buf, fields, way):
        for n, a in enumerate(fields):
            if way < 2:
                buf[way, n] = ld(xf, a * AREA + (2 if way == 0 else RI + 1) * XC + 8, CJ).astype(BF16)
            else:
                buf[way, n] = rows(a, 0, 0 if way == 2 else CJ - 1, 16).astype(BF16)

    for way, fields in enumerate((UP1, DOWN1, LEFT1, RIGHT1)):
        message(m_1, fields, way)
    for m, (di, dj, fields) in enumerate(CORNERS):
        for n, a in enumerate(fields):
            at = a * AREA + (2 + (0 if di < 0 else RI - 1)) * XC + 8 + (0 if dj < 0 else CJ - 1)
            m_co[m, n : n + 1] = ld(xf, at, 1)

    pl.semaphore_wait(barrier, len(partners))

    def remote(src, dst, ssem, rsem, to):
        return pltpu.make_async_remote_copy(
            src_ref=src, dst_ref=dst, send_sem=ssem, recv_sem=rsem, device_id=to, device_id_type=MESH
        )

    halo1, halo2 = [], []
    for m, (di, dj, _) in enumerate(CORNERS):
        halo1.append(remote(m_co.at[m], r_co.at[m], hs.at[m], hr.at[m], near(di, dj)))
    for way, fields in enumerate((UP1, DOWN1, LEFT1, RIGHT1)):
        n = len(fields)
        halo1.append(
            remote(m_1.at[way, :n], r_1.at[way, :n], hs.at[4 + way], hr.at[4 + way], near(*ways[way]))
        )
    for c in halo1:
        c.start()
    for c in loads[3:]:
        c.wait()

    def turn(t, carry):
        at = pl.multiple_of(t * CH, CH)
        convwt[pl.ds(at, CH), :] = convw[pl.ds(at, CH), :].T
        upwt[pl.ds(at, CH), :] = upw[pl.ds(at, CH), :].T
        return carry

    lax.fori_loop(0, 9, turn, 0)
    src = lax.broadcasted_iota(jnp.int32, (CH, CH), 0)
    dst = lax.broadcasted_iota(jnp.int32, (CH, CH), 1)
    wanted = (((dst % HL) // CB) * XL + dst // HL) * CB + dst % CB
    perm = jnp.where(src == wanted, 1.0, 0.0).astype(BF16)

    keep_top = jnp.where(band == 0, 0.0, 1.0)
    keep_bot = jnp.where(band == nband - 1, 0.0, 1.0)

    def receive(buf, fields, way):
        for n, a in enumerate(fields):
            value = buf[way, n].astype(F32)
            if way == 0:
                st(xf, a * AREA + (RI + 2) * XC + 8, CJ, value * keep_bot)
            elif way == 1:
                st(xf, a * AREA + XC + 8, CJ, value * keep_top)
            else:
                st(xf, a * AREA + 2 * XC + (8 + CJ if way == 2 else 7), RI, value[:RI], XC)

    for way, fields in enumerate((UP2, DOWN2, LEFT2, RIGHT2)):
        message(m_2, fields, way)
        n = len(fields)
        halo2.append(
            remote(m_2.at[way, :n], r_2.at[way, :n], hs.at[8 + way], hr.at[8 + way], near(*ways[way]))
        )
    def window(ref, a, i, dj, n):
        return jnp.concatenate(
            [ld(ref, a * AREA + (i + q + 2) * XC + 8 + dj, CJ) for q in range(n)], axis=0
        )

    def up(left, r, s):
        terms = []
        for k, di in ((1, 0),) if r == 0 else ((2, 0), (0, 1)):
            for l, dj in ((1, 0),) if s == 0 else ((2, 0), (0, 1)):
                terms.append((2 * di + dj, (3 * k + l) * CH))
        terms = [lambda n=n, at=at: dot(left[n], upw[at : at + CH, :]) for n, at in terms]
        return terms[0], sum((term() for term in terms[1:]), 0.0)

    def activate(r, s, pre):
        ph = 2 * r + s
        sig = jax.nn.sigmoid(pre)
        act = (pre * sig).astype(BF16).astype(F32)
        dfac[ph] = sig * (1.0 + pre * (1.0 - sig))
        for q in range(RI):
            st(af, ph * AREA + (q + 2) * XC + 8, CJ, act[16 * q : 16 * q + 16])
        actt[:, ph * 192 : ph * 192 + 192] = act.T.astype(BF16)

    ce[0] = window(xf, 0, 0, 0, RI).astype(BF16)
    cet[0] = window(xf, 0, 0, 0, RI).T.astype(BF16)
    for r in range(2):
        for s in range(2):
            ph = 2 * r + s
            at = (3 * (1 + r) + 1 + s) * CH
            own = dot(ce[0], upw[at : at + CH, :]) + window(xf, 1 + ph, 0, 0, RI)
            if ph:
                dfac[ph] = own
            else:
                activate(0, 0, own)
            tv[2 * ph] = window(xf, 5 + ph, -1, 0, 14).astype(BF16)
            tvp[2 * ph] = dot(tv[2 * ph], perm).astype(BF16)

    for c in halo1:
        c.wait()
    for c in halo2:
        c.start()
    for way, fields in enumerate((UP1, DOWN1, LEFT1, RIGHT1)):
        receive(r_1, fields, way)
    for m, (di, dj, fields) in enumerate(CORNERS):
        keep = keep_bot if di < 0 else keep_top
        for n, a in enumerate(fields):
            at = a * AREA + (RI + 2 if di < 0 else 1) * XC + (8 + CJ if dj < 0 else 7)
            st(xf, at, 1, r_co[m, n : n + 1] * keep)

    for n in range(1, 4):
        ce[n] = window(xf, 0, n // 2, n % 2, RI).astype(BF16)
    for r, s in ((0, 1), (1, 0), (1, 1)):
        activate(r, s, dfac[2 * r + s] + up(ce, r, s)[1])

    ends = []
    for ph in range(4):
        for i in (-1, RI):
            ends.append(window(xf, 5 + ph, i, 0, 1).astype(BF16))
            tv[2 * ph, 16 * (i + 1) : 16 * (i + 2)] = ends[-1]
    ends = dot(jnp.concatenate(ends, axis=0), perm).astype(BF16)
    for ph in range(4):
        for m, i in enumerate((-1, RI)):
            tvp[2 * ph, 16 * (i + 1) : 16 * (i + 2)] = ends[16 * (2 * ph + m) : 16 * (2 * ph + m + 1)]
        tv[2 * ph + 1] = window(xf, 5 + ph, -1, 1 if ph % 2 == 0 else -1, 14).astype(BF16)
        tvp[2 * ph + 1] = dot(tv[2 * ph + 1], perm).astype(BF16)

    def view(ref, er, es, i0, n):
        (r, di), (s, dj) = split(er), split(es)
        at = (i0 + di + 1) * 16
        return ref[(2 * r + s) * 2 + (1 if dj else 0), at : at + 16 * n]

    def put(arr, t, value):
        start = t * CH
        while start < (t + 1) * CH:
            f, off = divmod(start, FB)
            stop = min((t + 1) * CH, (f + 1) * FB)
            gsum[arr, f // (2 * Y), (f // 2) % Y, f % 2, off : off + stop - start] = value[
                start - t * CH : stop - t * CH
            ]
            start = stop

    def first(arr, a):
        c = remote(gsum.at[arr, a, :, 1 - core], r0.at[arr, a], s0s.at[arr, a], s0r.at[arr, a], at_core())
        c.start()
        return c

    step0c = []
    for t, (k, l) in enumerate(TAPS):
        right = jnp.concatenate(
            [view(tvp, r - k + 1, s - l + 1, 0, RI) for r in range(2) for s in range(2)], axis=0
        )
        put(0, t, dot(actt[...], right).astype(BF16))
        if XH == 2 and t == 6:
            step0c.append(first(0, 0))
    step0c.append(first(0, XH - 1))

    def half(x2):
        return pl.ds(pl.multiple_of(rem(x2, XL) * HL, HL), HL)

    def stage1(arr, arrived):
        steps = [[], []]
        for a in range(XH):
            arrived[a].wait()
            for b in range(Y):
                s1[arr, a, b] = gsum[arr, a, b, core] + r0[arr, a, b]
            for d in far_y:
                q = Y - d - 1
                steps[0].append(
                    remote(
                        s1.at[arr, a, rem(yy + d, Y), :RA], r1a.at[arr, q, a],
                        s1s.at[arr, a, d - 1], s1r.at[arr, a, q], at_y(d),
                    )
                )
                steps[0][-1].start()
        for d in far_x:
            q, x2 = NX - d - 1, rem(xx + d, NX)
            steps[1].append(
                remote(
                    s1.at[arr, div(x2, XL), :, RA:, half(x2)], r1b.at[arr, q],
                    s1s.at[arr, 2, d - 1], s1r.at[arr, 2, q], at_x(d),
                )
            )
            steps[1][-1].start()
        return steps

    phases = [(r, s) for r in range(2) for s in range(2)]

    def stacked(ref, step, group):
        return jnp.concatenate(
            [
                jnp.concatenate([view(ref, *step(r, s, k, l), 0, RI) for r, s in group], axis=0)
                for k, l in TAPS
            ],
            axis=1,
        )

    for g in range(0, 4, 4):
        group = phases[g : g + 4]
        left = stacked(tv, lambda r, s, k, l: (r - k + 1, s - l + 1), group)
        grads = dot(left, convwt[...])
        for n, (r, s) in enumerate(group):
            ph = 2 * r + s
            grad = (grads[192 * n : 192 * n + 192] * dfac[ph]).astype(BF16)
            gpp[ph] = dot(grad, perm).astype(BF16)
            gb[ph] = grad

    for n in range(1, 4):
        cet[n] = window(xf, 0, n // 2, n % 2, RI).T.astype(BF16)
    step1c = stage1(0, step0c)
    step0u = []
    for t, (k, l) in enumerate(TAPS):
        (r, di), (s, dj) = (((1, 1), (0, 0), (1, 0))[m] for m in (k, l))
        put(1, t, dot(cet[2 * di + dj], gpp[2 * r + s]).astype(BF16))
        if XH == 2 and t == 6:
            step0u.append(first(1, 0))
    step0u.append(first(1, XH - 1))

    def stage2a(arr, steps):
        for c in steps:
            c.wait()
        for a in range(XH):
            total = gsum[arr, a, yy, core, :RA].astype(F32) + r0[arr, a, yy, :RA].astype(F32)
            for d in range(Y - 1):
                total = total + r1a[arr, d, a].astype(F32)
            a1a[arr, a] = total
            s2a[arr, a] = total.astype(BF16)
        out = []
        for d in far_x:
            q, x2 = NX - d - 1, rem(xx + d, NX)
            out.append(
                remote(
                    s2a.at[arr, div(x2, XL), :, half(x2)], r2a.at[arr, q],
                    s2s.at[arr, 0, d - 1], s2r.at[arr, 0, q], at_x(d),
                )
            )
            out[-1].start()
        return out

    def stage2b(arr, steps):
        for c in steps:
            c.wait()
        own = half(xx)
        for b in range(Y):
            total = gsum[arr, xh, b, core, RA:, own].astype(F32) + r0[arr, xh, b, RA:, own].astype(F32)
            for d in range(NX - 1):
                total = total + r1b[arr, d, b].astype(F32)
            a1b[arr, b] = total
            s2b[arr, b] = total.astype(BF16)
        out = []
        for d in far_y:
            q = Y - d - 1
            out.append(
                remote(
                    s2b.at[arr, rem(yy + d, Y)], r2b.at[arr, q],
                    s2s.at[arr, 1, d - 1], s2r.at[arr, 1, q], at_y(d),
                )
            )
            out[-1].start()
        return out

    def stage3(arr, steps):
        for c in steps[0]:
            c.wait()
        total = a1a[arr, xh, :, half(xx)]
        for d in range(NX - 1):
            total = total + r2a[arr, d].astype(F32)
        pad[arr, :RA] = total
        for c in steps[1]:
            c.wait()
        total = a1b[arr, yy]
        for d in range(Y - 1):
            total = total + r2b[arr, d].astype(F32)
        pad[arr, RA:FB] = total
        turned = pad[arr].T
        for z in range(Z):
            a3[arr, z] = turned[z * CB : (z + 1) * CB]
            s3[arr, z] = turned[z * CB : (z + 1) * CB].astype(BF16)
        out = []
        for d in far_z:
            q = Z - d - 1
            out.append(
                remote(s3.at[arr, rem(zz + d, Z)], r3.at[arr, q], s3s.at[arr, d - 1], s3r.at[arr, q], at_z(d))
            )
            out[-1].start()
        return out

    def finish(arr, steps, out):
        for c in steps:
            c.wait()
        total = a3[arr, zz]
        for d in range(Z - 1):
            total = total + r3[arr, d].astype(F32)
        out[...] = total[:, :FB]

    def decode(group):
        outs = dot(stacked(av, lambda r, s, k, l: (r + k - 1, s + l - 1), group), convw[...])
        for n, (r, s) in enumerate(group):
            out = outs[192 * n : 192 * n + 192]
            for i in range(RI):
                st(dec_v, (2 * i + r) * 2 * CJ + s, CJ, out[16 * i : 16 * i + 16], 2)

    step1u = stage1(1, step0u)

    for c in halo2:
        c.wait()
    for way, fields in enumerate((UP2, DOWN2, LEFT2, RIGHT2)):
        receive(r_2, fields, way)

    def border(a, di, dj):
        return jnp.concatenate(
            [window(xf, a, di - 1, dj, 1), window(xf, a, di + RI, dj, 1)]
            + [rows(a, di - 1, dj - 1, 16), rows(a, di - 1, dj + CJ, 16)],
            axis=0,
        )

    for di in range(2):
        for dj in range(2):
            cg[2 * di + dj] = border(0, di, dj).astype(BF16)
    line = lax.broadcasted_iota(jnp.int32, (64, CH), 0)
    first_row = (line < 16) | ((line >= 32) & (line % 16 == 0))
    last_row = ((line >= 16) & (line < 32)) | ((line >= 32) & (line % 16 == RI + 1))
    ghost = ((band == 0) & first_row) | ((band == nband - 1) & last_row)
    for r in range(2):
        for s in range(2):
            ph = 2 * r + s
            own, others = up(cg, r, s)
            pre = own() + others + border(1 + ph, 0, 0)
            sig = jax.nn.sigmoid(pre)
            act = jnp.where(ghost, 0.0, pre * sig).astype(BF16).astype(F32)
            dghost[ph] = jnp.where(ghost, 0.0, sig * (1.0 + pre * (1.0 - sig)))
            st(af, ph * AREA + XC + 8, CJ, act[:16])
            st(af, ph * AREA + (RI + 2) * XC + 8, CJ, act[16:32])
            st(af, ph * AREA + XC + 7, 16, act[32:48], XC)
            st(af, ph * AREA + XC + 8 + CJ, 16, act[48:], XC)

    for s in range(2):
        for v, dj in enumerate((0, 1 if s == 0 else -1)):
            tv[2 * s + v, :16] = window(xf, 5 + s, -1, dj, 1).astype(BF16)

    for r in range(2):
        for s in range(2):
            for v, dj in enumerate((0, 1 if s == 0 else -1)):
                av[(2 * r + s) * 2 + v] = window(af, 2 * r + s, -1, dj, 14).astype(BF16)

    for ph in range(4):
        grad = gb[ph].astype(F32)
        for q in range(RI):
            st(gf, ph * AREA + (q + 2) * XC + 8, CJ, grad[16 * q : 16 * q + 16])
    lines, slopes = [], []
    for s in range(2):
        lines.append(jnp.concatenate([view(tv, 2 - k, s - l + 1, -1, 1) for k, l in TAPS], axis=1))
        slopes.append(dghost[2 + s, :16])
    for r in range(2):
        column = []
        for k, l in TAPS:
            (r2, di), (s2, dj) = split(r - k + 1), split(2 - l)
            column.append(rows(5 + 2 * r2 + s2, -1 + di, -1 + dj, 16).astype(BF16))
        lines.append(jnp.concatenate(column, axis=1))
        slopes.append(dghost[2 * r + 1, 32:48])
    grad = dot(jnp.concatenate(lines, axis=0), convwt[...]) * jnp.concatenate(slopes, axis=0)
    grad = grad.astype(BF16).astype(F32)
    st(gf, 2 * AREA + XC + 8, CJ, grad[:16])
    st(gf, 3 * AREA + XC + 8, CJ, grad[16:32])
    st(gf, AREA + XC + 7, 16, grad[32:48], XC)
    st(gf, 3 * AREA + XC + 7, 16, grad[48:], XC)
    for t, (k, l) in enumerate(TAPS):
        (r, di), (s, dj) = split(k - 1), split(l - 1)
        gv[:, t * CH : (t + 1) * CH] = window(gf, 2 * r + s, di, dj, RI).astype(BF16)

    decode(phases[0:4])
    gc_o[...] = dot(gv[...], upwt[...]).astype(BF16)
    for p in range(2 * RI):
        dec_o[p] = ld(dec_v, p * 2 * CJ, 2 * CJ).astype(BF16)

    step2c = [stage2a(0, step1c[0]), stage2b(0, step1c[1])]
    step2u = [stage2a(1, step1u[0]), stage2b(1, step1u[1])]
    step3c = stage3(0, step2c)
    step3u = stage3(1, step2u)
    finish(0, step3c, gw_o)
    finish(1, step3u, gu_o)


def deliver(*refs):
    n = (len(refs) - 1) // 2
    copies = [pltpu.make_async_copy(refs[i], refs[n + i], refs[-1].at[i]) for i in range(n)]
    for c in copies:
        c.start()
    for c in copies:
        c.wait()


def local(dims, coarse, skip, up_weight, conv_weight, cotangent):
    XH, Y, Z, XL = dims
    NX, HL = XH * XL, CH // XL
    FB, CB = 9 * CH // (XH * Y * 2), CH // (Z * XL)
    RA = FB // 16 * 4 // 9 * 16
    RB = FB - RA
    FP = -(-FB // 128) * 128
    hbm, vmem = pl.BlockSpec(memory_space=pltpu.HBM), pl.BlockSpec(memory_space=pltpu.VMEM)
    V, dma = pltpu.VMEM, pltpu.SemaphoreType.DMA
    wide = V((9 * CH, CH), BF16)
    scratch = [
        V((RI, CJ, CH), BF16), V((2 * RI, 2 * CJ, CH), BF16), V((2 * RI, 2 * CJ, CH), BF16),
        wide, wide, wide, wide,
        V((2, 9 * AREA, 128), F32), V((2, 4 * CJ, 128), F32), V((2, 4 * CJ, 128), F32),
        V((2, 4 * AREA, 128), F32), V((2, 4 * AREA, 128), F32), V((4, 192, CH), F32), V((4, 64, CH), F32),
        V((4, 192, CH), BF16), V((4, 64, CH), BF16), V((4, CH, 192), BF16), V((4, 192, CH), BF16), V((4, 192, CH), BF16),
        V((8, 224, CH), BF16), V((8, 224, CH), BF16), V((8, 224, CH), BF16),
        V((192, 9 * CH), BF16), V((CH, 768), BF16), V((2, 4 * RI * CJ, 128), F32),
        V((4, 3, 16, CH), BF16), V((4, 5, 16, CH), BF16), V((4, 8, CH), F32),
        V((4, 3, 16, CH), BF16), V((4, 5, 16, CH), BF16), V((4, 8, CH), F32),
        V((2, XH, Y, 2, FB, CH), BF16), V((2, XH, Y, FB, CH), BF16), V((2, XH, Y, FB, CH), BF16),
        V((2, Y - 1, XH, RA, CH), BF16), V((2, NX - 1, Y, RB, HL), BF16),
        V((2, XH, RA, CH), F32), V((2, Y, RB, HL), F32), V((2, XH, RA, CH), BF16), V((2, Y, RB, HL), BF16),
        V((2, NX - 1, RA, HL), BF16), V((2, Y - 1, RB, HL), BF16),
        V((2, FP, HL), F32), V((2, Z, CB, FP), F32), V((2, Z, CB, FP), BF16), V((2, Z - 1, CB, FP), BF16),
        dma((5,)), dma((12,)), dma((12,)), dma((2, 2)), dma((2, 2)),
        dma((2, 3, 3)), dma((2, 3, 3)), dma((2, 2, 3)), dma((2, 2, 3)), dma((2, Z - 1)), dma((2, Z - 1)),
    ]
    shapes = (
        jax.ShapeDtypeStruct((2 * RI, 2 * CJ, CH), BF16),
        jax.ShapeDtypeStruct((RI * CJ, CH), BF16),
        jax.ShapeDtypeStruct((CB, FB), F32),
        jax.ShapeDtypeStruct((CB, FB), F32),
    )
    inputs = (coarse, skip, up_weight.reshape(9 * CH, CH), conv_weight.reshape(9 * CH, CH), cotangent)
    inputs = [pltpu.with_memory_space_constraint(x, pltpu.HBM) for x in inputs]
    results = pl.pallas_call(
        functools.partial(kernel, dims),
        out_shape=shapes,
        in_specs=[hbm] * 5,
        out_specs=(vmem,) * 4,
        scratch_shapes=scratch,
        compiler_params=pltpu.CompilerParams(
            collective_id=0, has_side_effects=True, vmem_limit_bytes=36 * 2**20
        ),
    )(*inputs)
    decoded, grad_coarse, grad_up, grad_conv = pl.pallas_call(
        deliver,
        out_shape=shapes,
        in_specs=[vmem] * 4,
        out_specs=(hbm,) * 4,
        scratch_shapes=[dma((4,))],
        compiler_params=pltpu.CompilerParams(vmem_limit_bytes=4 * 2**20),
    )(*results)
    return decoded, grad_coarse.reshape(RI, CJ, CH), grad_up.T, grad_conv.T


def build(mesh, dims):
    cells = P("band", "face", None)
    return jax.shard_map(
        functools.partial(local, dims),
        mesh=mesh,
        in_specs=(cells, cells, P(), P(), cells),
        out_specs=(cells, cells, P("face", "band"), P("face", "band")),
        check_vma=False,
    )


def solution(mesh):
    return build(mesh, (2, 4, 8, 2))
```
